32 devices in a mesh: date: 16 (over z, y, core), strip: 2 (over x).
Axes of the slice: x: 2, y: 2, z: 4, core: 2. Of those that a mesh axis runs over, the one named last changes fastest.
Arguments:
- acquisitions: bfloat16 [32, 2, 2, 344, 640], P('date', None, None, None, 'strip'), may hold values from -6 to 6
- shifts: int32 [2, 32, 2, 5, 10], P(None, 'date', None, None, 'strip'), may hold values from -8 to 8, as said below
- fractions: int32 [2, 32, 2, 5, 10], P(None, 'date', None, None, 'strip'), may hold values from 0 to 63
- ref_dates: int32 [2], replicated, may hold values from 0 to 31, as said below
Outputs:
- chip_corr: float32 [2, 32, 2, 5, 10], P(None, 'date', None, None, 'strip')
- coherence: float32 [2, 31, 2, 64, 32], P(None, None, None, 'date', 'strip')
The draws below stay inside these ranges and needn't reach their ends.
Inputs may be any that keep to these rules, and one draw needn't show every extreme that they name: `shifts`: zero at every chip of date ref_dates[t] in tile t. `ref_dates`: the reference dates of consecutive tiles lie in different blocks of 2 dates.
All inputs are finite; a program needn't handle non-finite values.
Results may differ from the reference program's by a relative error of at most 0.0021.
Values may be sent and summed in bfloat16 or wider, within the bound.
A program may use at most 64 MiB of HBM per device.

```python
import jax
import jax.numpy as jnp
from jax import lax

DATE_DEV = 2
TILE_COUNT = 2
TILE_ROWS = 320
CHIP_SIZE = 64
MAX_SHIFT = 8
TAP_COUNT = 8
SUBSTEPS = 64
LOOK_AZ = 5
LOOK_RG = 20
DATE_COUNT = 32
TILE_COLS = 640
MARGIN = 12
CHIPS_AZ = 5
CHIPS_RG = 10
PAIR_COUNT = 31


def draw_layout(key):
    keys = jax.random.split(jax.random.fold_in(key, 11), 6)
    device_count = DATE_COUNT // DATE_DEV
    first_owner = jax.random.randint(keys[0], (), 0, device_count)
    stride = jax.random.randint(keys[1], (), 1, device_count)
    end_tile = jax.random.randint(keys[5], (), 0, TILE_COUNT)
    tile_axis = jnp.arange(TILE_COUNT, dtype=jnp.int32)
    base_owners = (first_owner + tile_axis * stride) % device_count
    owners = (base_owners - base_owners[end_tile] + device_count - 1) % device_count
    slot_pick = jax.random.randint(keys[2], (TILE_COUNT,), 0, DATE_DEV)
    slot_pick = jnp.where(tile_axis == end_tile, DATE_DEV - 1, slot_pick)
    ref_dates = (owners * DATE_DEV + slot_pick).astype(jnp.int32)
    baseline = jax.random.randint(keys[3], (2, DATE_COUNT, TILE_COUNT, 1, 1), 2 - MAX_SHIFT, MAX_SHIFT - 1)
    jitter = jax.random.randint(keys[4], (2, DATE_COUNT, TILE_COUNT, CHIPS_AZ, CHIPS_RG), -2, 3)
    is_reference = jnp.arange(DATE_COUNT, dtype=jnp.int32)[:, None] == ref_dates[None, :]
    shifts = jnp.where(is_reference[None, :, :, None, None], 0, baseline + jitter)
    return (ref_dates, shifts.astype(jnp.int32))


def draw_ref_dates(key, part):
    return draw_layout(key)[0]


def draw_shifts(key, part):
    return draw_layout(key)[1]


def draw_acquisitions(key, part):
    ref_dates, shifts = draw_layout(key)
    scene_key, noise_key = jax.random.split(jax.random.fold_in(key, 23))
    scene_shape = (TILE_COUNT, 2, TILE_ROWS + 2 * MARGIN + 2 * MAX_SHIFT, TILE_COLS + 2 * MAX_SHIFT)
    scene = jax.random.normal(scene_key, scene_shape, jnp.float32)
    line_rows = jnp.arange(TILE_ROWS + 2 * MARGIN, dtype=jnp.int32)
    line_cols = jnp.arange(TILE_COLS, dtype=jnp.int32)
    chip_rows = jnp.clip((line_rows - MARGIN) // CHIP_SIZE, 0, CHIPS_AZ - 1)
    chip_cols = line_cols // CHIP_SIZE
    tile_axis = jnp.arange(TILE_COUNT, dtype=jnp.int32)[:, None, None, None]
    part_axis = jnp.arange(2, dtype=jnp.int32)[None, :, None, None]

    def one_date(date_index):
        offsets = -lax.dynamic_index_in_dim(shifts, date_index, 1, keepdims=False)
        row_offsets = offsets[0][:, chip_rows[:, None], chip_cols[None, :]]
        col_offsets = offsets[1][:, chip_rows[:, None], chip_cols[None, :]]
        source_rows = line_rows[None, :, None] + row_offsets + MAX_SHIFT
        source_cols = line_cols[None, None, :] + col_offsets + MAX_SHIFT
        values = scene[tile_axis, part_axis, source_rows[:, None], source_cols[:, None]]
        date_key = jax.random.fold_in(noise_key, date_index)
        noise = 0.5 * jax.random.normal(date_key, values.shape, jnp.float32)
        return jnp.clip(values + noise, -6.0, 6.0)
    return lax.map(one_date, jnp.arange(DATE_COUNT, dtype=jnp.int32)).astype(jnp.bfloat16)


def touch_ends(drawn, rng, low, top_value):
    longest = drawn.shape.index(max(drawn.shape))
    spots = []
    for shift in (0, 1):
        where = [jax.random.randint(jax.random.fold_in(rng, axis), (), 0, length) for axis, length in enumerate(drawn.shape)]
        where[longest] = (where[longest] + shift) % drawn.shape[longest]
        spots.append(tuple(where))
    return drawn.at[spots[0]].set(low).at[spots[1]].set(top_value)


def setup_inputs(seed: int = 0) -> dict:
    streams_of = jax.random.split(jax.random.key(seed), 5)
    return {
        "acquisitions": draw_acquisitions(jax.random.fold_in(streams_of[4], 71), 0),
        "shifts": draw_shifts(jax.random.fold_in(streams_of[4], 71), 0),
        "fractions": touch_ends(jax.random.randint(streams_of[2], (2, DATE_COUNT, TILE_COUNT, CHIPS_AZ, CHIPS_RG), 0, SUBSTEPS), jax.random.fold_in(streams_of[2], 1), 0, SUBSTEPS - 1).astype(jnp.int32),
        "ref_dates": draw_ref_dates(jax.random.fold_in(streams_of[4], 71), 0),
    }


epsilon = 1e-06

def sinc_matrix(shift_part, fraction_part):
    window_size = CHIP_SIZE + 2 * MARGIN
    offset = fraction_part.astype(jnp.float32) / SUBSTEPS
    tap_axis = jnp.arange(TAP_COUNT).astype(jnp.float32)
    distance = tap_axis - (TAP_COUNT // 2 - 1) - offset[..., None]
    weights = jnp.sinc(distance) * (0.5 + 0.5 * jnp.cos(jnp.pi * distance / (TAP_COUNT // 2)))
    weights = weights / lax.optimization_barrier(jnp.sum(weights, axis=-1, keepdims=True))
    out_rows = jnp.arange(CHIP_SIZE, dtype=jnp.int32)[:, None]
    in_rows = jnp.arange(window_size, dtype=jnp.int32)[None, :]
    matrix = jnp.zeros(shift_part.shape + (CHIP_SIZE, window_size), jnp.float32)
    for tap_index in range(TAP_COUNT):
        target = out_rows + shift_part[..., None, None] + (tap_index - TAP_COUNT // 2 + 1 + MARGIN)
        matrix = matrix + jnp.where(in_rows == target, weights[..., tap_index][..., None, None], 0.0)
    return matrix.astype(jnp.bfloat16)

def correlate(reference_tiles, resampled):
    chips_az = resampled.shape[-2] // CHIP_SIZE
    chips_rg = resampled.shape[-1] // CHIP_SIZE

    def as_chips(values):
        return values.astype(jnp.float32).reshape(values.shape[:-2] + (chips_az, CHIP_SIZE, chips_rg, CHIP_SIZE))
    ref_chips = as_chips(reference_tiles)
    sec_chips = as_chips(resampled)
    ref_real = ref_chips[..., 0, :, :, :, :]
    ref_imag = ref_chips[..., 1, :, :, :, :]
    sec_real = sec_chips[..., 0, :, :, :, :]
    sec_imag = sec_chips[..., 1, :, :, :, :]
    cross_real = lax.optimization_barrier(jnp.sum(ref_real * sec_real + ref_imag * sec_imag, axis=(-3, -1)))
    cross_imag = lax.optimization_barrier(jnp.sum(ref_imag * sec_real - ref_real * sec_imag, axis=(-3, -1)))
    ref_power = lax.optimization_barrier(jnp.sum(ref_real * ref_real + ref_imag * ref_imag, axis=(-3, -1)))
    sec_power = lax.optimization_barrier(jnp.sum(sec_real * sec_real + sec_imag * sec_imag, axis=(-3, -1)))
    denominator = jnp.sqrt((ref_power + epsilon) * (sec_power + epsilon))
    return jnp.stack([cross_real / denominator, cross_imag / denominator])

def multilook_pairs(series):
    values = series.astype(jnp.float32)
    earlier = values[:-1]
    second = values[1:]
    early_real = earlier[:, :, 0]
    early_imag = earlier[:, :, 1]
    later_real = second[:, :, 0]
    later_imag = second[:, :, 1]
    cross_real = early_real * later_real + early_imag * later_imag
    cross_imag = early_imag * later_real - early_real * later_imag
    power_early = early_real * early_real + early_imag * early_imag
    power_later = later_real * later_real + later_imag * later_imag

    def box_sum(quantity):
        blocked = quantity.reshape(quantity.shape[:2] + (quantity.shape[2] // LOOK_AZ, LOOK_AZ, quantity.shape[3] // LOOK_RG, LOOK_RG))
        return lax.optimization_barrier(jnp.sum(blocked, axis=(3, 5)))
    denominator = jnp.sqrt((box_sum(power_early) + epsilon) * (box_sum(power_later) + epsilon))
    return jnp.stack([box_sum(cross_real) / denominator, box_sum(cross_imag) / denominator])

def reference(acquisitions, shifts, fractions, ref_dates):
    window_size = CHIP_SIZE + 2 * MARGIN
    padded = jnp.pad(acquisitions, ((0, 0), (0, 0), (0, 0), (0, 0), (MARGIN, MARGIN)))
    reference_tiles = jnp.stack([lax.dynamic_index_in_dim(acquisitions[:, tile_index], ref_dates[tile_index], 0, keepdims=False)[:, MARGIN:MARGIN + TILE_ROWS, :] for tile_index in range(TILE_COUNT)])
    row_index = (jnp.arange(CHIPS_AZ, dtype=jnp.int32) * CHIP_SIZE)[:, None] + jnp.arange(window_size, dtype=jnp.int32)[None, :]
    col_index = (jnp.arange(CHIPS_RG, dtype=jnp.int32) * CHIP_SIZE)[:, None] + jnp.arange(window_size, dtype=jnp.int32)[None, :]

    def one_date(date_index):
        date_frame = lax.dynamic_index_in_dim(padded, date_index, 0, keepdims=False)
        windows = date_frame[:, :, row_index[:, :, None, None], col_index[None, None, :, :]]
        windows = windows.transpose(0, 2, 4, 1, 3, 5).astype(jnp.float32)
        shift_now = lax.dynamic_index_in_dim(shifts, date_index, 1, keepdims=False)
        fraction_now = lax.dynamic_index_in_dim(fractions, date_index, 1, keepdims=False)
        azimuth = sinc_matrix(shift_now[0], fraction_now[0]).astype(jnp.float32)
        across = sinc_matrix(shift_now[1], fraction_now[1]).astype(jnp.float32)
        partial_rows = jnp.einsum('tariw,tarcwv->tarciv', azimuth, windows).astype(jnp.bfloat16)
        chips_out = jnp.einsum('tarciv,tarjv->tarcij', partial_rows.astype(jnp.float32), across).astype(jnp.bfloat16)
        resampled = chips_out.transpose(0, 3, 1, 4, 2, 5).reshape(TILE_COUNT, 2, TILE_ROWS, TILE_COLS)
        return (resampled, correlate(reference_tiles, resampled))
    resampled_all, corr_all = lax.map(one_date, jnp.arange(DATE_COUNT, dtype=jnp.int32))
    chip_corr = corr_all.transpose(1, 0, 2, 3, 4)

    def one_pair(pair_index):
        couple = lax.dynamic_slice_in_dim(resampled_all, pair_index, 2, 0)
        return multilook_pairs(couple)[:, 0]
    looked = lax.map(one_pair, jnp.arange(PAIR_COUNT, dtype=jnp.int32))
    coherence = looked.transpose(1, 0, 2, 3, 4)
    return (chip_corr, coherence)
```

```python
import functools

import jax
import jax.numpy as jnp
from jax import lax
from jax.experimental import pallas as pl
from jax.experimental.pallas import tpu as pltpu
from jax.sharding import PartitionSpec as P

CHIP_SIZE = 64
TAP_COUNT = 8
SUBSTEPS = 64
LOOK_AZ = 5
LOOK_RG = 20
MARGIN = 12
LANES = 128
GROUP = 8
PACK = 16
HALO = 16
WINDOW = 96
BAND = 160
CORES = 2
SIDES = 2

epsilon = 1e-06
MESH = pl.DeviceIdType.MESH


def tap_weights(k, fraction):
    distance = k.astype(jnp.float32) - (TAP_COUNT // 2 - 1) - fraction.astype(jnp.float32) / SUBSTEPS
    angle = jnp.pi * distance
    sinc = jnp.where(
        distance == 0.0, 1.0, jnp.sin(angle) / jnp.where(distance == 0.0, 1.0, angle)
    )
    weights = sinc * (0.5 + 0.5 * jnp.cos(jnp.pi * distance / (TAP_COUNT // 2)))
    weights = jnp.where((k >= 0) & (k < TAP_COUNT), weights, 0.0)
    return weights / jnp.sum(weights, axis=1, keepdims=True)


def spread(row, count, start):
    tall = jnp.broadcast_to(row, (count, LANES))
    return pltpu.roll(tall, start, 1, stride=1, stride_axis=0)


def split_dot(values, selector):
    high = values.astype(jnp.bfloat16)
    low = (values - high.astype(jnp.float32)).astype(jnp.bfloat16)
    return jnp.dot(high, selector, preferred_element_type=jnp.float32) + jnp.dot(
        low, selector, preferred_element_type=jnp.float32
    )


def kernel(
    n, strips, dims,
    frame_hbm, shifts_hbm, fractions_hbm, dates_hbm,
    coh_ref, corr_ref,
    frame, shifts_ref, fractions_ref, dates_ref, spots, line_base, col_base,
    cand, core_in, y_out, y_in, z_out, z_in, whole,
    series, sent, got, cross_sums, powers, selectors, out_buf, coh_in, ordered, totals,
    load_sem, small_sem, edge_send, edge_recv, core_send, core_recv, y_send, y_recv,
    z_send, z_recv, next_send, next_recv, coh_send, coh_recv,
):
    tiles, kept, chips_az, chips_rg, rows, cols = dims
    me = lax.axis_index("date")
    strip = lax.axis_index("strip")
    core = me % CORES
    side = (me // CORES) % SIDES
    levels = n // (CORES * SIDES)
    level = me // (CORES * SIDES)
    bf16 = jnp.bfloat16
    f32 = jnp.float32
    chips = chips_az * chips_rg
    chip_units = CHIP_SIZE // PACK
    half_chips = -(-chips // SIDES)
    half_units = whole.shape[2]
    piece = half_units // levels
    steps = [levels // 2] + [o for o in range(1, levels) if o != levels // 2]

    def at_level(o):
        return lax.rem(level + o, levels)

    def device(z, y, c):
        return {"date": (z * SIDES + y) * CORES + c}

    def remote(src, dst, send, recv, where):
        return pltpu.make_async_remote_copy(
            src_ref=src, dst_ref=dst, send_sem=send, recv_sem=recv,
            device_id=where, device_id_type=MESH,
        )

    inner = pl.ds(HALO, cols)
    loads = {}
    for i, (d, t) in enumerate(((core, 1 - core), (1 - core, 1 - core), (core, core), (1 - core, core))):
        loads[i] = pltpu.make_async_copy(
            frame_hbm.at[d, t], frame.at[d, t, :, inner, :], load_sem.at[i]
        )
        loads[i].start()
    smalls = [
        pltpu.make_async_copy(src, dst, small_sem.at[i])
        for i, (src, dst) in enumerate(
            ((shifts_hbm, shifts_ref), (fractions_hbm, fractions_ref), (dates_hbm, dates_ref))
        )
    ]
    for copy in smalls:
        copy.start()

    barrier = pltpu.get_barrier_semaphore()
    for o in range(1, n):
        pl.semaphore_signal(
            barrier, inc=1, device_id={"date": lax.rem(me + o, n)}, device_id_type=MESH
        )
    has_low = strip > 0
    has_high = strip < strips - 1

    @pl.when(has_low)
    def _():
        pl.semaphore_signal(barrier, inc=1, device_id={"strip": strip - 1}, device_id_type=MESH)

    @pl.when(has_high)
    def _():
        pl.semaphore_signal(barrier, inc=1, device_id={"strip": strip + 1}, device_id_type=MESH)

    edge_zero = jnp.zeros((kept, tiles, 2, HALO, frame.shape[4]), bf16)

    @pl.when(strip == 0)
    def _():
        frame[:, :, :, 0:HALO, :] = edge_zero

    @pl.when(strip == strips - 1)
    def _():
        frame[:, :, :, HALO + cols : 2 * HALO + cols, :] = edge_zero

    lane = lax.broadcasted_iota(jnp.int32, (GROUP, LANES), 1)

    def wide(count):
        return lax.broadcasted_iota(jnp.int32, (count, LANES), 1)

    for copy in smalls:
        copy.wait()

    for d in range(kept):
        for a in range(chips_az):
            row = (d * chips_az + a) * tiles
            for i in range(2):
                spots[i, row : row + tiles, :chips_rg] = shifts_ref[i, d, a]
                spots[2 + i, row : row + tiles, :chips_rg] = fractions_ref[i, d, a]
    spot_rows = kept * chips_az * tiles
    first_tap = MARGIN - TAP_COUNT // 2 + 1
    at = wide(spot_rows)
    for r in range(chips_rg):
        values = [
            jnp.broadcast_to(spots[i, 0:spot_rows, r : r + 1], (spot_rows, LANES)) for i in range(4)
        ]
        line_tap = ((LANES - at) & (LANES - 1)) - (values[0] + first_tap)
        line_base[r, 0:spot_rows, :] = tap_weights(line_tap, values[2])
        col_tap = at - (values[1] + (first_tap + HALO - MARGIN))
        col_base[r, 0:spot_rows, :] = tap_weights(col_tap, values[3])

    for y in range(SIDES):
        used = (min(chips, (y + 1) * half_chips) - y * half_chips) * chip_units
        if used < half_units:
            for t in range(tiles):
                cand[t, y, used:half_units] = jnp.zeros((half_units - used, PACK, LANES), bf16)

    dates_row = dates_ref[0:1, :]

    def pick(t):
        def body(r, carry):
            at = wide(CHIP_SIZE)
            low = at < CHIP_SIZE
            inside = at >= MARGIN
            date_lane = lax.broadcasted_iota(jnp.int32, (1, tiles), 1)
            date = jnp.sum(jnp.where(date_lane == t, dates_row, 0), axis=1, keepdims=True)
            here = pl.ds(pl.multiple_of(HALO + r * CHIP_SIZE, PACK), CHIP_SIZE)
            parts = []
            for c in range(2):
                total = None
                for d in range(kept):
                    gain = jnp.where(date == me * kept + d, 1.0, 0.0).astype(f32)
                    value = frame[d, t, c, here, :].astype(f32) * gain
                    total = value if total is None else total + value
                blocks = []
                for b in range(-(-total.shape[1] // LANES)):
                    block = total[:, b * LANES : min((b + 1) * LANES, total.shape[1])]
                    if block.shape[1] < LANES:
                        block = jnp.concatenate(
                            [block, jnp.zeros((CHIP_SIZE, LANES - block.shape[1]), f32)], axis=1
                        )
                    blocks.append(block)
                parts.append(blocks)
            for a in range(chips_az):
                b = a // 2
                moves = (LANES - MARGIN, CHIP_SIZE - MARGIN)
                pair = [p[b] for p in parts]
                if a % 2:
                    moves = moves[::-1]
                    pair = [jnp.where(inside, p[b], p[b + 1]) for p in parts]
                pair = [pltpu.roll(v, m, 1) for v, m in zip(pair, moves)]
                mixed = jnp.where(low, pair[0], pair[1]).astype(bf16)
                chip = a * chips_rg + r
                unit = (chip % half_chips) * chip_units
                cand[t, chip // half_chips, pl.ds(unit, chip_units)] = mixed.reshape(
                    chip_units, PACK, LANES
                )
            return carry

        lax.fori_loop(0, chips_rg, body, 0)

    loads[0].wait()
    loads[1].wait()
    pick(1 - core)

    beside = jnp.minimum(strip, 1) + jnp.minimum(strips - 1 - strip, 1)
    pl.semaphore_wait(barrier, n - 1 + beside)

    core_rs = [
        remote(cand.at[1 - core, y], core_in.at[y], core_send.at[i], core_recv.at[i],
               device(level, side, 1 - core))
        for i, y in enumerate((1 - side, side))
    ]
    for copy in core_rs:
        copy.start()

    order = ((core, core), (1 - core, 1 - core), (core, 1 - core), (1 - core, core))
    edges = []
    for i, (d, t) in enumerate(order):
        up = remote(
            frame_hbm.at[d, t, :, pl.ds(cols - HALO, HALO), :], frame.at[d, t, :, pl.ds(0, HALO), :],
            edge_send.at[0, i], edge_recv.at[0, i], {"strip": strip + 1},
        )
        down = remote(
            frame_hbm.at[d, t, :, pl.ds(0, HALO), :], frame.at[d, t, :, pl.ds(HALO + cols, HALO), :],
            edge_send.at[1, i], edge_recv.at[1, i], {"strip": strip - 1},
        )
        edges.append((up, down))

        @pl.when(has_high)
        def _():
            up.start()

        @pl.when(has_low)
        def _():
            down.start()

    def edge_wait(i):
        @pl.when(has_low)
        def _():
            edges[i][0].wait_recv()

        @pl.when(has_high)
        def _():
            edges[i][1].wait_recv()

    loads[2].wait()
    loads[3].wait()
    pick(core)

    def level_piece(z):
        return pl.ds(z * piece, piece)

    y_rs = [
        remote(y_out.at[level_piece(at_level(o))], y_in.at[k], y_send.at[0, k], y_recv.at[0, k],
               device(level, 1 - side, core))
        for k, o in enumerate(steps + [0])
    ]
    z_rs = [
        remote(z_out.at[k], z_in.at[k], z_send.at[0, k], z_recv.at[0, k],
               device(at_level(o), side, core))
        for k, o in enumerate(steps)
    ]
    mine = whole.at[core, side, level_piece(level)]
    z_ag = [
        remote(mine, mine, z_send.at[1, k], z_recv.at[1, k], device(at_level(o), side, core))
        for k, o in enumerate(steps)
    ]
    y_ag = []
    for k, o in enumerate(steps + [0]):
        part = whole.at[core, side, level_piece(at_level(levels - o))]
        y_ag.append(
            remote(part, part, y_send.at[1, k], y_recv.at[1, k], device(level, 1 - side, core))
        )
    core_ag = [
        remote(whole.at[core, y], whole.at[core, y], core_send.at[2 + i], core_recv.at[2 + i],
               device(level, side, 1 - core))
        for i, y in enumerate((side, 1 - side))
    ]

    def ref_core():
        core_rs[0].wait_recv()
        y_out[...] = cand[core, 1 - side] + core_in[1 - side]
        for copy in y_rs:
            copy.start()

    def piece_sum(k, o):
        at = level_piece(at_level(o))
        y_rs[k].wait_recv()
        return cand[core, side, at] + core_in[side, at] + y_in[k]

    def ref_side(k):
        if k == 0:
            core_rs[1].wait_recv()
        z_out[k] = piece_sum(k, steps[k])
        z_rs[k].start()

    def ref_level():
        total = piece_sum(len(steps), 0)
        for k in range(len(steps)):
            z_rs[k].wait_recv()
            total = total + z_in[k]
        whole[core, side, level_piece(level)] = total
        for copy in z_ag:
            copy.start()
        y_ag[len(steps)].start()

    def ref_back(k):
        z_ag[k].wait_recv()
        y_ag[k].start()
        if k == len(steps) - 1:
            core_ag[0].start()

    def ref_other():
        for copy in y_ag:
            copy.wait_recv()
        core_ag[1].start()

    low_lane = wide(CHIP_SIZE) < CHIP_SIZE

    def halves(count):
        return wide(count) < CHIP_SIZE

    def chip_column(d, t, r, slot):
        row0 = pl.multiple_of(r * CHIP_SIZE, CHIP_SIZE)
        window = pl.ds(row0, WINDOW)

        def base(ref, a):
            return ref[r, pl.ds((d * chips_az + a) * tiles + t, 1), :]

        partial = [None] * chips_az
        reach = CHIP_SIZE + 2 * MARGIN
        for a in range(0, chips_az - 1, 2):
            b = a // 2
            span = slice(b * LANES, b * LANES + BAND)
            image = jnp.concatenate([frame[d, t, c, window, span] for c in range(2)], axis=0)
            first = spread(base(line_base, a), reach, 0)
            second = spread(base(line_base, a + 1), BAND - CHIP_SIZE, CHIP_SIZE)
            shared = reach - CHIP_SIZE
            matrix = jnp.concatenate(
                [
                    jnp.where(halves(CHIP_SIZE), first[:CHIP_SIZE], 0.0),
                    jnp.where(halves(shared), first[CHIP_SIZE:], second[:shared]),
                    jnp.where(halves(BAND - reach), 0.0, second[shared:]),
                ],
                axis=0,
            ).astype(bf16)
            out = jnp.dot(image, matrix, preferred_element_type=f32)
            re, im = out[:WINDOW], out[WINDOW:]
            left = halves(WINDOW)
            partial[a] = jnp.where(left, re, pltpu.roll(im, CHIP_SIZE, 1)).astype(bf16)
            partial[a + 1] = jnp.where(left, pltpu.roll(re, CHIP_SIZE, 1), im).astype(bf16)
        if chips_az % 2:
            a = chips_az - 1
            span = slice(a * CHIP_SIZE, a * CHIP_SIZE + reach)
            row = base(line_base, a)
            left = halves(reach)
            top = jnp.where(left, spread(row, reach, 0), 0.0).astype(bf16)
            bottom = jnp.where(left, 0.0, spread(row, reach, CHIP_SIZE)).astype(bf16)
            partial[a] = (
                jnp.dot(frame[d, t, 0, window, span], top, preferred_element_type=f32)
                + jnp.dot(frame[d, t, 1, window, span], bottom, preferred_element_type=f32)
            ).astype(bf16)
        for a in range(chips_az):
            matrix = spread(base(col_base, a), CHIP_SIZE, 0)[:, :WINDOW].astype(bf16)
            out = jnp.dot(matrix, partial[a], preferred_element_type=f32).astype(bf16)
            if slot is not None:
                unit = (a * chips_rg + r) * chip_units
                sent[slot, pl.ds(unit, chip_units)] = out.reshape(chip_units, PACK, LANES)
            out = out.astype(f32)
            series[t, d + t, a, pl.ds(row0, CHIP_SIZE), :] = out
            power = jnp.sum((out * out).reshape(GROUP, GROUP, LANES), axis=0)
            totals[1 + 2 * kept + d, r, pl.ds((a * tiles + t) * GROUP, GROUP), :] = power

    def resample(i, first, last):
        d, t = order[i]

        def body(j, carry):
            chip_column(d, t, lax.rem(j + 1, chips_rg), i if i < 2 else None)
            return carry

        lax.fori_loop(first, last, body, 0)

    inside_cols = chips_rg - 2
    peer = me + 2 * core - 1
    has_peer = (peer >= 0) & (peer < n)
    outward = remote(sent.at[0], got.at[0], next_send.at[0], next_recv.at[0], {"date": peer})
    inward = remote(
        sent.at[1], got.at[1], next_send.at[1], next_recv.at[1], device(level, side, 1 - core)
    )

    resample(0, 0, 1)
    ref_core()
    resample(0, 1, inside_cols)
    edge_wait(0)
    resample(0, inside_cols, chips_rg)

    @pl.when(has_peer)
    def _():
        outward.start()

    ref_side(0)
    resample(1, 0, inside_cols)
    edge_wait(1)
    resample(1, inside_cols, chips_rg)
    inward.start()
    ref_side(1)
    edge_wait(2)
    resample(2, 0, chips_rg)
    for k in range(2, len(steps)):
        ref_side(k)
    edge_wait(3)
    resample(3, 0, chips_rg)

    looks_rg = cols // LOOK_RG
    look_rows = rows // LOOK_AZ

    def pick_rows(t, pos, a, s):
        return series[t, pos, a, pl.ds(s, looks_rg, stride=LOOK_RG), :]

    def look(t, early, wanted):
        def body(a, carry):
            sums = [jnp.zeros((looks_rg, LANES), f32) for _ in range(2 + len(wanted))]
            for s in range(LOOK_RG):
                first = pick_rows(t, early, a, s)
                second = pick_rows(t, early + 1, a, s)
                sums[0] = sums[0] + first * second
                sums[1] = sums[1] + first * pltpu.roll(second, CHIP_SIZE, 1)
                for i, pos in enumerate(wanted):
                    value = pick_rows(t, pos, a, s)
                    sums[2 + i] = sums[2 + i] + value * value
            span = pl.ds(pl.multiple_of(a * LANES, LANES), LANES)
            row = pl.multiple_of((early * tiles + t) * looks_rg, GROUP)
            for c in range(2):
                cross_sums[c, pl.ds(row, looks_rg), span] = sums[c]
            for i, pos in enumerate(wanted):
                row = pl.multiple_of((pos * tiles + t) * looks_rg, GROUP)
                powers[pl.ds(row, looks_rg), span] = sums[2 + i]
            return carry

        lax.fori_loop(0, chips_az, body, 0)

    def unpack(i, t, pos):
        def body(j, carry):
            for a in range(chips_az):
                unit = a * chips_rg * chip_units + j * chip_units
                value = got[i, pl.ds(unit, chip_units)].reshape(CHIP_SIZE, LANES)
                row = pl.multiple_of(j * CHIP_SIZE, CHIP_SIZE)
                series[t, pos, a, pl.ds(row, CHIP_SIZE), :] = value.astype(f32)
            return carry

        lax.fori_loop(0, chips_rg, body, 0)

    look(0, 0, (0, 1))
    look(1, 1, (1, 2))

    def build_selectors(a, carry):
        line = lax.broadcasted_iota(jnp.int32, (LANES, LANES), 0)
        y = lax.broadcasted_iota(jnp.int32, (LANES, LANES), 1)
        gap = a * CHIP_SIZE + (line & (CHIP_SIZE - 1)) - LOOK_AZ * y
        hit = (gap >= 0) & (gap < LOOK_AZ)
        span = pl.ds(pl.multiple_of(a * LANES, LANES), LANES)
        selectors[0, span, :] = jnp.where(hit, 1.0, 0.0).astype(bf16)
        selectors[1, span, :] = jnp.where(
            hit, jnp.where(line < CHIP_SIZE, -1.0, 1.0), 0.0
        ).astype(bf16)
        return carry

    lax.fori_loop(0, chips_az, build_selectors, 0)

    inward.wait_recv()
    unpack(1, core, 2 * (1 - core))
    look(core, 1 - core, (2 * (1 - core),))
    ref_level()

    @pl.when(has_peer)
    def _():
        outward.wait_recv()
        unpack(0, 1 - core, 2 * core)

    @pl.when(jnp.logical_not(has_peer))
    def _():
        series[1 - core, 2 * core] = jnp.zeros(series.shape[2:], f32)

    look(1 - core, core, (2 * core,))

    summed = [split_dot(cross_sums[c], selectors[c]) for c in range(2)]
    power = split_dot(powers[...], selectors[0])
    count = kept * tiles * looks_rg
    skip = tiles * looks_rg
    scale = jnp.sqrt((power[:count] + epsilon) * (power[skip : skip + count] + epsilon))
    coherence = jnp.concatenate([v / scale for v in summed], axis=0).T
    share = look_rows // n
    for j in range(n):
        out_buf[j] = coherence[j * share : (j + 1) * share]
    coh_in[me] = out_buf[me]
    relays = []
    for o in range(1, n):
        to = lax.rem(me + o, n)
        copy = remote(
            out_buf.at[to], coh_in.at[me], coh_send.at[o], coh_recv.at[o], {"date": to}
        )
        copy.start()
        relays.append(copy)

    for k in range(len(steps)):
        ref_back(k)

    def correlate(t, y):
        def body(j, carry):
            chip = y * half_chips + j
            a = chip // chips_rg
            r = chip % chips_rg
            ref = whole[t, y, pl.ds(j * chip_units, chip_units)]
            ref = ref.reshape(CHIP_SIZE, LANES).astype(f32)
            turned = pltpu.roll(ref, CHIP_SIZE, 1)
            row = pl.multiple_of(r * CHIP_SIZE, CHIP_SIZE)
            to = pl.ds(pl.multiple_of((a * tiles + t) * GROUP, GROUP), GROUP)

            def put(k, value):
                total = jnp.sum(value.reshape(GROUP, GROUP, LANES), axis=0)
                totals[k, r, to, :] = total

            put(0, ref * ref)
            for d in range(kept):
                value = series[t, d + t, a, pl.ds(row, CHIP_SIZE), :]
                put(1 + 2 * d, ref * value)
                put(2 + 2 * d, turned * value)
            return carry

        lax.fori_loop(0, jnp.minimum(half_chips, chips - y * half_chips), body, 0)

    correlate(core, side)
    ref_other()
    correlate(core, 1 - side)
    core_ag[0].wait_recv()
    correlate(1 - core, side)
    core_ag[1].wait_recv()
    correlate(1 - core, 1 - side)

    kinds = totals.shape[0]
    group_rows = totals.shape[2] // GROUP
    lane16 = wide(group_rows)
    sign = jnp.where(lane16 < CHIP_SIZE, 1.0, -1.0).astype(f32)
    folded = []
    for k in range(kinds):
        line = []
        for r in range(chips_rg):
            total = None
            for s in range(GROUP):
                value = totals[k, r, pl.ds(s, group_rows, stride=GROUP), :]
                total = value if total is None else total + value
            if 1 <= k <= 2 * kept and k % 2 == 0:
                total = total * sign
            line.append(total)
        folded.append(jnp.concatenate(line, axis=1))
    folded = jnp.concatenate(folded, axis=0)
    depth = chips_rg * LANES
    source = lax.broadcasted_iota(jnp.int32, (depth, LANES), 0)
    target = lax.broadcasted_iota(jnp.int32, (depth, LANES), 1)
    gap = source - target * LANES
    gather = jnp.where((gap >= 0) & (gap < LANES), 1.0, 0.0).astype(bf16)
    sums = split_dot(folded, gather)
    sums = [sums[k * group_rows : (k + 1) * group_rows] for k in range(kinds)]
    for d in range(kept):
        scale = jnp.sqrt((sums[0] + epsilon) * (sums[1 + 2 * kept + d] + epsilon))
        for c in range(2):
            value = sums[1 + 2 * d + c] / scale
            for a in range(chips_az):
                corr_ref[c, d, a] = value[a * tiles : (a + 1) * tiles, :chips_rg]

    for copy in relays:
        copy.wait_recv()
    pairs = n * kept
    lane_n = wide(n)
    for y in range(share):
        value = coh_in[:, y, :]
        ordered[y, pl.ds(0, n, stride=2), :] = value
        ordered[y, pl.ds(1, n, stride=2), :] = pltpu.roll(value, LANES - tiles * looks_rg, 1)
    lane_p = wide(pairs)
    for y in range(share):
        first = (lane_p & (2 * looks_rg - 1)) < looks_rg
        value = jnp.where(first, ordered[y, 0:pairs, :], ordered[y, 1 : pairs + 1, :]).T
        for c in range(2):
            for t in range(tiles):
                row = c * kept * tiles * looks_rg + t * looks_rg
                coh_ref[c, t, y] = value[row : row + looks_rg, : pairs - 1]

    for copy in relays + core_rs + y_rs + z_rs + z_ag + y_ag + core_ag + [inward]:
        copy.wait_send()

    @pl.when(has_peer)
    def _():
        outward.wait_send()

    for up, down in edges:
        @pl.when(has_high)
        def _():
            up.wait_send()

        @pl.when(has_low)
        def _():
            down.wait_send()


def per_device(n, strips, acquisitions, shifts, fractions, ref_dates):
    kept, tiles, _, all_rows, cols = acquisitions.shape
    rows = all_rows - 2 * MARGIN
    chips_az, chips_rg = shifts.shape[3:]
    chips = chips_az * chips_rg
    units = chips * CHIP_SIZE // PACK
    levels = n // (CORES * SIDES)
    half_chips = -(-chips // SIDES)
    piece = -(-(half_chips * CHIP_SIZE // PACK) // levels)
    half_units = piece * levels
    looks_rg = cols // LOOK_RG
    look_rows = rows // LOOK_AZ
    share = look_rows // n
    spot_rows = -(-(kept * chips_az * tiles) // GROUP) * GROUP
    group_rows = -(-(chips_az * tiles) // GROUP) * GROUP
    kinds = 1 + 3 * kept
    f32 = jnp.float32
    bf16 = jnp.bfloat16
    dma = pltpu.SemaphoreType.DMA
    vmem = pl.BlockSpec(memory_space=pltpu.VMEM)
    frames = jnp.swapaxes(acquisitions, 3, 4)
    order = (0, 1, 3, 2, 4)
    coh, corr = pl.pallas_call(
        functools.partial(kernel, n, strips, (tiles, kept, chips_az, chips_rg, rows, cols)),
        out_shape=(
            jax.ShapeDtypeStruct((2, tiles, share, looks_rg, n * kept - 1), f32),
            jax.ShapeDtypeStruct((2, kept, chips_az, tiles, chips_rg), f32),
        ),
        in_specs=[pl.BlockSpec(memory_space=pl.ANY)] * 4,
        out_specs=(vmem, vmem),
        scratch_shapes=[
            pltpu.VMEM((kept, tiles, 2, cols + 2 * HALO, all_rows), bf16),
            pltpu.VMEM((2, kept, chips_az, tiles, chips_rg), jnp.int32),
            pltpu.VMEM((2, kept, chips_az, tiles, chips_rg), jnp.int32),
            pltpu.VMEM((1, tiles), jnp.int32),
            pltpu.VMEM((4, spot_rows, LANES), jnp.int32),
            pltpu.VMEM((chips_rg, spot_rows, LANES), f32),
            pltpu.VMEM((chips_rg, spot_rows, LANES), f32),
            pltpu.VMEM((tiles, SIDES, half_units, PACK, LANES), bf16),
            pltpu.VMEM((SIDES, half_units, PACK, LANES), bf16),
            pltpu.VMEM((half_units, PACK, LANES), bf16),
            pltpu.VMEM((levels, piece, PACK, LANES), bf16),
            pltpu.VMEM((levels - 1, piece, PACK, LANES), bf16),
            pltpu.VMEM((levels - 1, piece, PACK, LANES), bf16),
            pltpu.VMEM((tiles, SIDES, half_units, PACK, LANES), bf16),
            pltpu.VMEM((tiles, kept + 1, chips_az, cols, LANES), f32),
            pltpu.VMEM((2, units, PACK, LANES), bf16),
            pltpu.VMEM((2, units, PACK, LANES), bf16),
            pltpu.VMEM((2, kept * tiles * looks_rg, chips_az * LANES), f32),
            pltpu.VMEM(((kept + 1) * tiles * looks_rg, chips_az * LANES), f32),
            pltpu.VMEM((2, chips_az * LANES, LANES), bf16),
            pltpu.VMEM((n, share, LANES), f32),
            pltpu.VMEM((n, share, LANES), f32),
            pltpu.VMEM((share, n * kept + GROUP, LANES), f32),
            pltpu.VMEM((kinds, chips_rg, group_rows * GROUP, LANES), f32),
            dma((4,)), dma((3,)), dma((2, 4)), dma((2, 4)), dma((4,)), dma((4,)),
            dma((2, levels)), dma((2, levels)), dma((2, levels - 1)), dma((2, levels - 1)),
            dma((2,)), dma((2,)), dma((n,)), dma((n,)),
        ],
        compiler_params=pltpu.CompilerParams(
            collective_id=0, has_side_effects=True, vmem_limit_bytes=50 * 1024 * 1024
        ),
    )(frames, shifts.transpose(order), fractions.transpose(order), ref_dates[None])
    return (corr.transpose(order), coh.transpose(0, 4, 1, 2, 3))


def solution(mesh):
    return jax.shard_map(
        functools.partial(per_device, mesh.shape["date"], mesh.shape["strip"]),
        mesh=mesh,
        in_specs=(
            P("date", None, None, None, "strip"),
            P(None, "date", None, None, "strip"),
            P(None, "date", None, None, "strip"),
            P(),
        ),
        out_specs=(P(None, "date", None, None, "strip"), P(None, None, None, "date", "strip")),
        check_vma=False,
    )
```

```python
import functools

import jax
import jax.numpy as jnp
from jax import lax
from jax.experimental import pallas as pl
from jax.experimental.pallas import tpu as pltpu
from jax.sharding import PartitionSpec as P

CHIP_SIZE = 64
TAP_COUNT = 8
SUBSTEPS = 64
LOOK_AZ = 5
LOOK_RG = 20
MARGIN = 12
LANES = 128
GROUP = 8
PACK = 16
HALO = 16
WINDOW = 96
BAND = 160
CORES = 2
SIDES = 2

epsilon = 1e-06
COS_TERMS = (1.0, -1 / 2, 1 / 24, -1 / 720, 1 / 40320, -1 / 3628800, 1 / 479001600, -1 / 87178291200)
MESH = pl.DeviceIdType.MESH


def half_turn_cos(square):
    total = jnp.full(square.shape, COS_TERMS[-1], jnp.float32)
    for term in COS_TERMS[-2::-1]:
        total = total * square + term
    return total


def tap_weights(k, fraction):
    part = fraction.astype(jnp.float32) / SUBSTEPS
    distance = k.astype(jnp.float32) - (TAP_COUNT // 2 - 1) - part
    turn = (part - 0.5) * jnp.pi
    sine = half_turn_cos(turn * turn)
    sine = jnp.where((k & 1) == 0, sine, -sine)
    sine = jnp.where(part == 0.0, 0.0, sine)
    angle = jnp.pi * distance
    sinc = jnp.where(distance == 0.0, 1.0, sine / jnp.where(distance == 0.0, 1.0, angle))
    eighth = distance * (jnp.pi / TAP_COUNT)
    window = half_turn_cos(eighth * eighth)
    weights = sinc * (window * window)
    weights = jnp.where((k >= 0) & (k < TAP_COUNT), weights, 0.0)
    return weights / jnp.sum(weights, axis=1, keepdims=True)


def spread(row, count, start):
    tall = jnp.broadcast_to(row, (count, LANES))
    return pltpu.roll(tall, start, 1, stride=1, stride_axis=0)


def split_dot(values, selector):
    high = values.astype(jnp.bfloat16)
    low = (values - high.astype(jnp.float32)).astype(jnp.bfloat16)
    return jnp.dot(high, selector, preferred_element_type=jnp.float32) + jnp.dot(
        low, selector, preferred_element_type=jnp.float32
    )


def kernel(
    n, strips, dims,
    frame_hbm, shifts_hbm, fractions_hbm, dates_hbm,
    coh_ref, corr_ref,
    frame, shifts_ref, fractions_ref, dates_ref, spots, line_base, col_base,
    cand, core_in, y_out, y_in, z_out, z_in, whole,
    series, sent, got, cross_sums, powers, selectors, out_buf, coh_in, ordered, totals,
    load_sem, small_sem, edge_send, edge_recv, core_send, core_recv, y_send, y_recv,
    z_send, z_recv, next_send, next_recv, coh_send, coh_recv,
):
    tiles, kept, chips_az, chips_rg, rows, cols = dims
    me = lax.axis_index("date")
    strip = lax.axis_index("strip")
    core = me % CORES
    side = (me // CORES) % SIDES
    levels = n // (CORES * SIDES)
    level = me // (CORES * SIDES)
    bf16 = jnp.bfloat16
    f32 = jnp.float32
    chips = chips_az * chips_rg
    chip_units = CHIP_SIZE // PACK
    half_chips = -(-chips // SIDES)
    half_units = whole.shape[2]
    piece = half_units // levels
    steps = [levels // 2] + [o for o in range(1, levels) if o != levels // 2]

    def at_level(o):
        return lax.rem(level + o, levels)

    def device(z, y, c):
        return {"date": (z * SIDES + y) * CORES + c}

    def remote(src, dst, send, recv, where):
        return pltpu.make_async_remote_copy(
            src_ref=src, dst_ref=dst, send_sem=send, recv_sem=recv,
            device_id=where, device_id_type=MESH,
        )

    inner = pl.ds(HALO, cols)
    loads = {}
    for i, (d, t) in enumerate(((core, 1 - core), (1 - core, 1 - core), (core, core), (1 - core, core))):
        loads[i] = pltpu.make_async_copy(
            frame_hbm.at[d, t], frame.at[d, t, :, inner, :], load_sem.at[i]
        )
        loads[i].start()
    smalls = [
        pltpu.make_async_copy(src, dst, small_sem.at[i])
        for i, (src, dst) in enumerate(
            ((shifts_hbm, shifts_ref), (fractions_hbm, fractions_ref), (dates_hbm, dates_ref))
        )
    ]
    for copy in smalls:
        copy.start()

    barrier = pltpu.get_barrier_semaphore()
    for o in range(1, n):
        pl.semaphore_signal(
            barrier, inc=1, device_id={"date": lax.rem(me + o, n)}, device_id_type=MESH
        )
    has_low = strip > 0
    has_high = strip < strips - 1

    @pl.when(has_low)
    def _():
        pl.semaphore_signal(barrier, inc=1, device_id={"strip": strip - 1}, device_id_type=MESH)

    @pl.when(has_high)
    def _():
        pl.semaphore_signal(barrier, inc=1, device_id={"strip": strip + 1}, device_id_type=MESH)

    edge_zero = jnp.zeros((kept, tiles, 2, HALO, frame.shape[4]), bf16)

    @pl.when(strip == 0)
    def _():
        frame[:, :, :, 0:HALO, :] = edge_zero

    @pl.when(strip == strips - 1)
    def _():
        frame[:, :, :, HALO + cols : 2 * HALO + cols, :] = edge_zero

    lane = lax.broadcasted_iota(jnp.int32, (GROUP, LANES), 1)

    def wide(count):
        return lax.broadcasted_iota(jnp.int32, (count, LANES), 1)

    for y in range(SIDES):
        used = (min(chips, (y + 1) * half_chips) - y * half_chips) * chip_units
        if used < half_units:
            for t in range(tiles):
                cand[t, y, used:half_units] = jnp.zeros((half_units - used, PACK, LANES), bf16)


    def move(depth, start, c):
        source = lax.broadcasted_iota(jnp.int32, (depth, LANES), 0)
        target = lax.broadcasted_iota(jnp.int32, (depth, LANES), 1)
        mine = (target < CHIP_SIZE) if c == 0 else (target >= CHIP_SIZE)
        hit = mine & (source == target - c * CHIP_SIZE + start)
        return jnp.where(hit, 1.0, 0.0).astype(bf16)

    def pick(t):
        dates_row = dates_ref[0:1, :]
        date_lane = lax.broadcasted_iota(jnp.int32, (1, tiles), 1)
        date = jnp.sum(jnp.where(date_lane == t, dates_row, 0), axis=1, keepdims=True)
        gains = [
            jnp.broadcast_to(jnp.where(date == me * kept + d, 1.0, 0.0), (cols, frame.shape[4]))
            .astype(bf16)
            for d in range(kept)
        ]
        even = [move(LANES, MARGIN, c) for c in range(2)]
        odd = [move(BAND, MARGIN + CHIP_SIZE, c) for c in range(2)]

        parts = []
        for c in range(2):
            total = frame[0, t, c, inner, :] * gains[0]
            for d in range(1, kept):
                total = total + frame[d, t, c, inner, :] * gains[d]
            parts.append(total)
        for a in range(chips_az):
            start = (a // 2) * LANES
            depth = min(BAND if a % 2 else LANES, frame.shape[4] - start)
            mixed = sum(
                jnp.dot(
                    parts[c][:, start : start + depth],
                    (odd if a % 2 else even)[c][:depth],
                    preferred_element_type=f32,
                )
                for c in range(2)
            ).astype(bf16)
            for r in range(chips_rg):
                chip = a * chips_rg + r
                unit = (chip % half_chips) * chip_units
                value = mixed[r * CHIP_SIZE : (r + 1) * CHIP_SIZE]
                cand[t, chip // half_chips, unit : unit + chip_units] = value.reshape(
                    chip_units, PACK, LANES
                )

    smalls[2].wait()
    loads[0].wait()
    loads[1].wait()
    pick(1 - core)

    beside = jnp.minimum(strip, 1) + jnp.minimum(strips - 1 - strip, 1)
    pl.semaphore_wait(barrier, n - 1 + beside)

    core_rs = [
        remote(cand.at[1 - core, y], core_in.at[y], core_send.at[i], core_recv.at[i],
               device(level, side, 1 - core))
        for i, y in enumerate((1 - side, side))
    ]
    for copy in core_rs:
        copy.start()

    order = ((core, core), (1 - core, 1 - core), (core, 1 - core), (1 - core, core))
    edges = []
    for i, (d, t) in enumerate(order):
        up = remote(
            frame_hbm.at[d, t, :, pl.ds(cols - HALO, HALO), :], frame.at[d, t, :, pl.ds(0, HALO), :],
            edge_send.at[0, i], edge_recv.at[0, i], {"strip": strip + 1},
        )
        down = remote(
            frame_hbm.at[d, t, :, pl.ds(0, HALO), :], frame.at[d, t, :, pl.ds(HALO + cols, HALO), :],
            edge_send.at[1, i], edge_recv.at[1, i], {"strip": strip - 1},
        )
        edges.append((up, down))

        @pl.when(has_high)
        def _():
            up.start()

        @pl.when(has_low)
        def _():
            down.start()

    def edge_wait(i):
        @pl.when(has_low)
        def _():
            edges[i][0].wait_recv()

        @pl.when(has_high)
        def _():
            edges[i][1].wait_recv()

    smalls[0].wait()
    smalls[1].wait()

    for d in range(kept):
        for a in range(chips_az):
            row = (d * chips_az + a) * tiles
            for i in range(2):
                spots[i, row : row + tiles, :chips_rg] = shifts_ref[i, d, a]
                spots[2 + i, row : row + tiles, :chips_rg] = fractions_ref[i, d, a]
    spot_rows = kept * chips_az * tiles
    first_tap = MARGIN - TAP_COUNT // 2 + 1
    at = wide(spot_rows)
    for r in range(chips_rg):
        values = [
            jnp.broadcast_to(spots[i, 0:spot_rows, r : r + 1], (spot_rows, LANES)) for i in range(4)
        ]
        line_tap = ((LANES - at) & (LANES - 1)) - (values[0] + first_tap)
        line_base[r, 0:spot_rows, :] = tap_weights(line_tap, values[2])
        col_tap = at - (values[1] + (first_tap + HALO - MARGIN))
        col_base[r, 0:spot_rows, :] = tap_weights(col_tap, values[3])

    loads[2].wait()
    loads[3].wait()
    pick(core)

    def level_piece(z):
        return pl.ds(z * piece, piece)

    y_rs = [
        remote(y_out.at[level_piece(at_level(o))], y_in.at[k], y_send.at[0, k], y_recv.at[0, k],
               device(level, 1 - side, core))
        for k, o in enumerate(steps + [0])
    ]
    z_rs = [
        remote(z_out.at[k], z_in.at[k], z_send.at[0, k], z_recv.at[0, k],
               device(at_level(o), side, core))
        for k, o in enumerate(steps)
    ]
    mine = whole.at[core, side, level_piece(level)]
    z_ag = [
        remote(mine, mine, z_send.at[1, k], z_recv.at[1, k], device(at_level(o), side, core))
        for k, o in enumerate(steps)
    ]
    y_ag = []
    for k, o in enumerate(steps + [0]):
        part = whole.at[core, side, level_piece(at_level(levels - o))]
        y_ag.append(
            remote(part, part, y_send.at[1, k], y_recv.at[1, k], device(level, 1 - side, core))
        )
    core_ag = [
        remote(whole.at[core, y], whole.at[core, y], core_send.at[2 + i], core_recv.at[2 + i],
               device(level, side, 1 - core))
        for i, y in enumerate((side, 1 - side))
    ]

    def ref_core():
        core_rs[0].wait_recv()
        y_out[...] = cand[core, 1 - side] + core_in[1 - side]
        for copy in y_rs:
            copy.start()

    def piece_sum(k, o):
        at = level_piece(at_level(o))
        y_rs[k].wait_recv()
        return cand[core, side, at] + core_in[side, at] + y_in[k]

    def ref_side(k):
        if k == 0:
            core_rs[1].wait_recv()
        z_out[k] = piece_sum(k, steps[k])
        z_rs[k].start()

    def ref_level():
        total = piece_sum(len(steps), 0)
        for k in range(len(steps)):
            z_rs[k].wait_recv()
            total = total + z_in[k]
        whole[core, side, level_piece(level)] = total
        for copy in z_ag:
            copy.start()
        y_ag[len(steps)].start()

    def ref_back(k):
        z_ag[k].wait_recv()
        y_ag[k].start()
        if k == len(steps) - 1:
            core_ag[0].start()

    def ref_other():
        for copy in y_ag:
            copy.wait_recv()
        core_ag[1].start()

    low_lane = wide(CHIP_SIZE) < CHIP_SIZE

    def halves(count):
        return wide(count) < CHIP_SIZE

    def chip_column(d, t, r, slot):
        row0 = r * CHIP_SIZE
        window = pl.ds(row0, WINDOW)

        def base(ref, a):
            return ref[r, pl.ds((d * chips_az + a) * tiles + t, 1), :]

        partial = [None] * chips_az
        reach = CHIP_SIZE + 2 * MARGIN
        for a in range(0, chips_az - 1, 2):
            b = a // 2
            span = slice(b * LANES, b * LANES + BAND)
            image = jnp.concatenate([frame[d, t, c, window, span] for c in range(2)], axis=0)
            first = spread(base(line_base, a), reach, 0)
            second = spread(base(line_base, a + 1), BAND - CHIP_SIZE, CHIP_SIZE)
            shared = reach - CHIP_SIZE
            matrix = jnp.concatenate(
                [
                    jnp.where(halves(CHIP_SIZE), first[:CHIP_SIZE], 0.0),
                    jnp.where(halves(shared), first[CHIP_SIZE:], second[:shared]),
                    jnp.where(halves(BAND - reach), 0.0, second[shared:]),
                ],
                axis=0,
            ).astype(bf16)
            out = jnp.dot(image, matrix, preferred_element_type=f32)
            re, im = out[:WINDOW], out[WINDOW:]
            left = halves(WINDOW)
            partial[a] = jnp.where(left, re, pltpu.roll(im, CHIP_SIZE, 1)).astype(bf16)
            partial[a + 1] = jnp.where(left, pltpu.roll(re, CHIP_SIZE, 1), im).astype(bf16)
        if chips_az % 2:
            a = chips_az - 1
            span = slice(a * CHIP_SIZE, a * CHIP_SIZE + reach)
            row = base(line_base, a)
            left = halves(reach)
            top = jnp.where(left, spread(row, reach, 0), 0.0).astype(bf16)
            bottom = jnp.where(left, 0.0, spread(row, reach, CHIP_SIZE)).astype(bf16)
            partial[a] = (
                jnp.dot(frame[d, t, 0, window, span], top, preferred_element_type=f32)
                + jnp.dot(frame[d, t, 1, window, span], bottom, preferred_element_type=f32)
            ).astype(bf16)
        for a in range(chips_az):
            matrix = spread(base(col_base, a), CHIP_SIZE, 0)[:, :WINDOW].astype(bf16)
            out = jnp.dot(matrix, partial[a], preferred_element_type=f32).astype(bf16)
            if slot is not None:
                unit = (a * chips_rg + r) * chip_units
                sent[slot, pl.ds(unit, chip_units)] = out.reshape(chip_units, PACK, LANES)
            out = out.astype(f32)
            series[t, d + t, a, pl.ds(row0, CHIP_SIZE), :] = out
            power = jnp.sum((out * out).reshape(GROUP, GROUP, LANES), axis=0)
            totals[1 + 2 * kept + d, r, pl.ds((a * tiles + t) * GROUP, GROUP), :] = power

    def resample(i, first, last):
        d, t = order[i]

        for j in range(first, last):
            chip_column(d, t, (j + 1) % chips_rg, i if i < 2 else None)

    inside_cols = chips_rg - 2
    peer = me + 2 * core - 1
    has_peer = (peer >= 0) & (peer < n)
    outward = remote(sent.at[0], got.at[0], next_send.at[0], next_recv.at[0], {"date": peer})
    inward = remote(
        sent.at[1], got.at[1], next_send.at[1], next_recv.at[1], device(level, side, 1 - core)
    )

    ref_core()
    resample(0, 0, inside_cols)
    edge_wait(0)
    resample(0, inside_cols, chips_rg)

    @pl.when(has_peer)
    def _():
        outward.start()

    resample(1, 0, inside_cols)
    edge_wait(1)
    resample(1, inside_cols, chips_rg)
    inward.start()
    ref_side(0)
    resample(2, 0, inside_cols)
    ref_side(1)
    edge_wait(2)
    resample(2, inside_cols, chips_rg)
    for k in range(2, len(steps)):
        ref_side(k)
    edge_wait(3)
    resample(3, 0, chips_rg)

    looks_rg = cols // LOOK_RG
    look_rows = rows // LOOK_AZ

    def pick_rows(t, pos, a, s):
        return series[t, pos, a, pl.ds(s, looks_rg, stride=LOOK_RG), :]

    def look(t, early, wanted):
        for a in range(chips_az):
            sums = [jnp.zeros((looks_rg, LANES), f32) for _ in range(2 + len(wanted))]
            for s in range(LOOK_RG):
                first = pick_rows(t, early, a, s)
                second = pick_rows(t, early + 1, a, s)
                sums[0] = sums[0] + first * second
                sums[1] = sums[1] + first * pltpu.roll(second, CHIP_SIZE, 1)
                for i, pos in enumerate(wanted):
                    value = pick_rows(t, pos, a, s)
                    sums[2 + i] = sums[2 + i] + value * value
            span = slice(a * LANES, (a + 1) * LANES)
            row = pl.multiple_of((early * tiles + t) * looks_rg, GROUP)
            for c in range(2):
                cross_sums[c, pl.ds(row, looks_rg), span] = sums[c]
            for i, pos in enumerate(wanted):
                row = pl.multiple_of((pos * tiles + t) * looks_rg, GROUP)
                powers[pl.ds(row, looks_rg), span] = sums[2 + i]

    def unpack(i, t, pos):
        def body(j, carry):
            for a in range(chips_az):
                unit = a * chips_rg * chip_units + j * chip_units
                value = got[i, pl.ds(unit, chip_units)].reshape(CHIP_SIZE, LANES)
                row = pl.multiple_of(j * CHIP_SIZE, CHIP_SIZE)
                series[t, pos, a, pl.ds(row, CHIP_SIZE), :] = value.astype(f32)
            return carry

        lax.fori_loop(0, chips_rg, body, 0)

    look(0, 0, (0, 1))
    look(1, 1, (1, 2))

    def build_selectors(a, carry):
        line = lax.broadcasted_iota(jnp.int32, (LANES, LANES), 0)
        y = lax.broadcasted_iota(jnp.int32, (LANES, LANES), 1)
        gap = a * CHIP_SIZE + (line & (CHIP_SIZE - 1)) - LOOK_AZ * y
        hit = (gap >= 0) & (gap < LOOK_AZ)
        span = pl.ds(pl.multiple_of(a * LANES, LANES), LANES)
        selectors[0, span, :] = jnp.where(hit, 1.0, 0.0).astype(bf16)
        selectors[1, span, :] = jnp.where(
            hit, jnp.where(line < CHIP_SIZE, -1.0, 1.0), 0.0
        ).astype(bf16)
        return carry

    lax.fori_loop(0, chips_az, build_selectors, 0)

    def correlate(t, y):
        for j in reversed(range(half_chips)):
            chip = jnp.minimum(y * half_chips + j, chips - 1)
            a = chip // chips_rg
            r = chip % chips_rg
            row = pl.multiple_of(r * CHIP_SIZE, CHIP_SIZE)
            to = pl.ds(pl.multiple_of((a * tiles + t) * GROUP, GROUP), GROUP)
            sums = [None] * (1 + 2 * kept)
            for g in range(chip_units):
                ref = whole[t, y, j * chip_units + g].astype(f32)
                turned = pltpu.roll(ref, CHIP_SIZE, 1)
                terms = [ref * ref]
                for d in range(kept):
                    value = series[t, d + t, a, pl.ds(row + g * PACK, PACK), :]
                    terms += [ref * value, turned * value]
                for k, term in enumerate(terms):
                    term = term[:GROUP] + term[GROUP:]
                    sums[k] = term if sums[k] is None else sums[k] + term
            for k, value in enumerate(sums):
                totals[k, r, to, :] = value

    inward.wait_recv()
    unpack(1, core, 2 * (1 - core))
    look(core, 1 - core, (2 * (1 - core),))
    ref_level()
    for k in range(len(steps)):
        ref_back(k)
    correlate(core, side)

    @pl.when(has_peer)
    def _():
        outward.wait_recv()
        unpack(0, 1 - core, 2 * core)

    @pl.when(jnp.logical_not(has_peer))
    def _():
        series[1 - core, 2 * core] = jnp.zeros(series.shape[2:], f32)

    look(1 - core, core, (2 * core,))

    summed = [split_dot(cross_sums[c], selectors[c]) for c in range(2)]
    power = split_dot(powers[...], selectors[0])
    count = kept * tiles * looks_rg
    skip = tiles * looks_rg
    scale = jnp.sqrt((power[:count] + epsilon) * (power[skip : skip + count] + epsilon))
    coherence = jnp.concatenate([v / scale for v in summed], axis=0).T
    share = look_rows // n
    for j in range(n):
        out_buf[j] = coherence[j * share : (j + 1) * share]
    coh_in[me] = out_buf[me]
    relays = []
    for o in range(1, n):
        to = lax.rem(me + o, n)
        copy = remote(
            out_buf.at[to], coh_in.at[me], coh_send.at[o], coh_recv.at[o], {"date": to}
        )
        copy.start()
        relays.append(copy)

    ref_other()
    correlate(core, 1 - side)
    core_ag[0].wait_recv()
    correlate(1 - core, side)
    core_ag[1].wait_recv()
    correlate(1 - core, 1 - side)

    kinds = totals.shape[0]
    group_rows = totals.shape[2] // GROUP
    lane16 = wide(group_rows)
    sign = jnp.where(lane16 < CHIP_SIZE, 1.0, -1.0).astype(f32)
    folded = []
    for k in range(kinds):
        line = []
        for r in range(chips_rg):
            total = None
            for s in range(GROUP):
                value = totals[k, r, pl.ds(s, group_rows, stride=GROUP), :]
                total = value if total is None else total + value
            if 1 <= k <= 2 * kept and k % 2 == 0:
                total = total * sign
            line.append(total)
        folded.append(jnp.concatenate(line, axis=1))
    folded = jnp.concatenate(folded, axis=0)
    depth = chips_rg * LANES
    source = lax.broadcasted_iota(jnp.int32, (depth, LANES), 0)
    target = lax.broadcasted_iota(jnp.int32, (depth, LANES), 1)
    gap = source - target * LANES
    gather = jnp.where((gap >= 0) & (gap < LANES), 1.0, 0.0).astype(bf16)
    sums = split_dot(folded, gather)
    sums = [sums[k * group_rows : (k + 1) * group_rows] for k in range(kinds)]
    for d in range(kept):
        scale = jnp.sqrt((sums[0] + epsilon) * (sums[1 + 2 * kept + d] + epsilon))
        for c in range(2):
            value = sums[1 + 2 * d + c] / scale
            for a in range(chips_az):
                corr_ref[c, d, a] = value[a * tiles : (a + 1) * tiles, :chips_rg]

    for copy in relays:
        copy.wait_recv()
    pairs = n * kept
    lane_n = wide(n)
    for y in range(share):
        value = coh_in[:, y, :]
        ordered[y, pl.ds(0, n, stride=2), :] = value
        ordered[y, pl.ds(1, n, stride=2), :] = pltpu.roll(value, LANES - tiles * looks_rg, 1)
    lane_p = wide(pairs)
    for y in range(share):
        first = (lane_p & (2 * looks_rg - 1)) < looks_rg
        value = jnp.where(first, ordered[y, 0:pairs, :], ordered[y, 1 : pairs + 1, :]).T
        for c in range(2):
            for t in range(tiles):
                row = c * kept * tiles * looks_rg + t * looks_rg
                coh_ref[c, t, y] = value[row : row + looks_rg, : pairs - 1]

    for copy in relays + core_rs + y_rs + z_rs + z_ag + y_ag + core_ag + [inward]:
        copy.wait_send()

    @pl.when(has_peer)
    def _():
        outward.wait_send()

    for up, down in edges:
        @pl.when(has_high)
        def _():
            up.wait_send()

        @pl.when(has_low)
        def _():
            down.wait_send()


def per_device(n, strips, acquisitions, shifts, fractions, ref_dates):
    kept, tiles, _, all_rows, cols = acquisitions.shape
    rows = all_rows - 2 * MARGIN
    chips_az, chips_rg = shifts.shape[3:]
    chips = chips_az * chips_rg
    units = chips * CHIP_SIZE // PACK
    levels = n // (CORES * SIDES)
    half_chips = -(-chips // SIDES)
    piece = -(-(half_chips * CHIP_SIZE // PACK) // levels)
    half_units = piece * levels
    looks_rg = cols // LOOK_RG
    look_rows = rows // LOOK_AZ
    share = look_rows // n
    spot_rows = -(-(kept * chips_az * tiles) // GROUP) * GROUP
    group_rows = -(-(chips_az * tiles) // GROUP) * GROUP
    kinds = 1 + 3 * kept
    f32 = jnp.float32
    bf16 = jnp.bfloat16
    dma = pltpu.SemaphoreType.DMA
    vmem = pl.BlockSpec(memory_space=pltpu.VMEM)
    frames = jnp.swapaxes(acquisitions, 3, 4)
    order = (0, 1, 3, 2, 4)
    coh, corr = pl.pallas_call(
        functools.partial(kernel, n, strips, (tiles, kept, chips_az, chips_rg, rows, cols)),
        out_shape=(
            jax.ShapeDtypeStruct((2, tiles, share, looks_rg, n * kept - 1), f32),
            jax.ShapeDtypeStruct((2, kept, chips_az, tiles, chips_rg), f32),
        ),
        in_specs=[pl.BlockSpec(memory_space=pltpu.HBM)] * 4,
        out_specs=(vmem, vmem),
        scratch_shapes=[
            pltpu.VMEM((kept, tiles, 2, cols + 2 * HALO, all_rows), bf16),
            pltpu.VMEM((2, kept, chips_az, tiles, chips_rg), jnp.int32),
            pltpu.VMEM((2, kept, chips_az, tiles, chips_rg), jnp.int32),
            pltpu.VMEM((1, tiles), jnp.int32),
            pltpu.VMEM((4, spot_rows, LANES), jnp.int32),
            pltpu.VMEM((chips_rg, spot_rows, LANES), f32),
            pltpu.VMEM((chips_rg, spot_rows, LANES), f32),
            pltpu.VMEM((tiles, SIDES, half_units, PACK, LANES), bf16),
            pltpu.VMEM((SIDES, half_units, PACK, LANES), bf16),
            pltpu.VMEM((half_units, PACK, LANES), bf16),
            pltpu.VMEM((levels, piece, PACK, LANES), bf16),
            pltpu.VMEM((levels - 1, piece, PACK, LANES), bf16),
            pltpu.VMEM((levels - 1, piece, PACK, LANES), bf16),
            pltpu.VMEM((tiles, SIDES, half_units, PACK, LANES), bf16),
            pltpu.VMEM((tiles, kept + 1, chips_az, cols, LANES), f32),
            pltpu.VMEM((2, units, PACK, LANES), bf16),
            pltpu.VMEM((2, units, PACK, LANES), bf16),
            pltpu.VMEM((2, kept * tiles * looks_rg, chips_az * LANES), f32),
            pltpu.VMEM(((kept + 1) * tiles * looks_rg, chips_az * LANES), f32),
            pltpu.VMEM((2, chips_az * LANES, LANES), bf16),
            pltpu.VMEM((n, share, LANES), f32),
            pltpu.VMEM((n, share, LANES), f32),
            pltpu.VMEM((share, n * kept + GROUP, LANES), f32),
            pltpu.VMEM((kinds, chips_rg, group_rows * GROUP, LANES), f32),
            dma((4,)), dma((3,)), dma((2, 4)), dma((2, 4)), dma((4,)), dma((4,)),
            dma((2, levels)), dma((2, levels)), dma((2, levels - 1)), dma((2, levels - 1)),
            dma((2,)), dma((2,)), dma((n,)), dma((n,)),
        ],
        compiler_params=pltpu.CompilerParams(
            collective_id=0, has_side_effects=True, vmem_limit_bytes=50 * 1024 * 1024
        ),
    )(*[pltpu.with_memory_space_constraint(v, pltpu.HBM) for v in (frames, shifts.transpose(order), fractions.transpose(order), ref_dates[None])])
    return (corr.transpose(order), coh.transpose(0, 4, 1, 2, 3))


def solution(mesh):
    return jax.shard_map(
        functools.partial(per_device, mesh.shape["date"], mesh.shape["strip"]),
        mesh=mesh,
        in_specs=(
            P("date", None, None, None, "strip"),
            P(None, "date", None, None, "strip"),
            P(None, "date", None, None, "strip"),
            P(),
        ),
        out_specs=(P(None, "date", None, None, "strip"), P(None, None, None, "date", "strip")),
        check_vma=False,
    )
```

```python
import functools

import jax
import jax.numpy as jnp
from jax import lax
from jax.experimental import pallas as pl
from jax.experimental.pallas import tpu as pltpu
from jax.sharding import PartitionSpec as P

CHIP_SIZE = 64
TAP_COUNT = 8
SUBSTEPS = 64
LOOK_AZ = 5
LOOK_RG = 20
MARGIN = 12
LANES = 128
GROUP = 8
PACK = 16
HALO = 16
WINDOW = 96
BAND = 160
CORES = 2
SIDES = 2
EARLY = 2
SHARE = 36

epsilon = 1e-06
COS_TERMS = (1.0, -1 / 2, 1 / 24, -1 / 720, 1 / 40320, -1 / 3628800, 1 / 479001600, -1 / 87178291200)
MESH = pl.DeviceIdType.MESH


def half_turn_cos(square):
    total = jnp.full(square.shape, COS_TERMS[-1], jnp.float32)
    for term in COS_TERMS[-2::-1]:
        total = total * square + term
    return total


def tap_weights(k, fraction):
    part = fraction.astype(jnp.float32) / SUBSTEPS
    distance = k.astype(jnp.float32) - (TAP_COUNT // 2 - 1) - part
    turn = (part - 0.5) * jnp.pi
    sine = half_turn_cos(turn * turn)
    sine = jnp.where((k & 1) == 0, sine, -sine)
    sine = jnp.where(part == 0.0, 0.0, sine)
    angle = jnp.pi * distance
    sinc = jnp.where(distance == 0.0, 1.0, sine / jnp.where(distance == 0.0, 1.0, angle))
    eighth = distance * (jnp.pi / TAP_COUNT)
    window = half_turn_cos(eighth * eighth)
    weights = sinc * (window * window)
    weights = jnp.where((k >= 0) & (k < TAP_COUNT), weights, 0.0)
    return weights / jnp.sum(weights, axis=1, keepdims=True)


def spread(row, count, start):
    tall = jnp.broadcast_to(row, (count, LANES))
    return pltpu.roll(tall, start, 1, stride=1, stride_axis=0)


def split_dot(values, selector):
    high = values.astype(jnp.bfloat16)
    low = (values - high.astype(jnp.float32)).astype(jnp.bfloat16)
    return jnp.dot(high, selector, preferred_element_type=jnp.float32) + jnp.dot(
        low, selector, preferred_element_type=jnp.float32
    )


def kernel(
    n, strips, dims,
    frame_hbm, shifts_hbm, fractions_hbm, dates_hbm,
    coh_ref, corr_ref,
    frame, shifts_ref, fractions_ref, dates_ref, spots, line_base, col_base,
    cand, core_in, y_out, y_in, z_out, z_in, across_out, across_in, over, over_in, whole,
    series, sent, got, cross_sums, powers, selectors, out_buf, coh_in, ordered, totals,
    load_sem, small_sem, edge_send, edge_recv, core_send, core_recv, y_send, y_recv,
    z_send, z_recv, side_recv, back_recv, next_send, next_recv, coh_send, coh_recv,
):
    tiles, kept, chips_az, chips_rg, rows, cols = dims
    me = lax.axis_index("date")
    strip = lax.axis_index("strip")
    core = me % CORES
    side = (me // CORES) % SIDES
    levels = n // (CORES * SIDES)
    level = me // (CORES * SIDES)
    bf16 = jnp.bfloat16
    f32 = jnp.float32
    chips = chips_az * chips_rg
    chip_units = CHIP_SIZE // PACK
    piece, strip_piece = y_in.shape[1], across_in.shape[1]
    half_units = levels * piece
    half_chips = half_units // chip_units
    tail_first = SIDES * half_chips
    tail = pl.ds(SIDES * half_units, levels * strip_piece)
    steps = [levels // 2] + [o for o in range(1, levels) if o != levels // 2]

    def at_level(o):
        return lax.rem(level + o, levels)

    def device(z, y, c):
        return {"date": (z * SIDES + y) * CORES + c}

    def remote(src, dst, send, recv, where):
        return pltpu.make_async_remote_copy(
            src_ref=src, dst_ref=dst, send_sem=send, recv_sem=recv,
            device_id=where, device_id_type=MESH,
        )

    inner = pl.ds(HALO, cols)
    dates_copy = pltpu.make_async_copy(dates_hbm, dates_ref, small_sem.at[0])
    dates_copy.start()
    loads = []
    for i, t in enumerate((1 - core, core)):
        loads.append(
            pltpu.make_async_copy(
                frame_hbm.at[:, t], frame.at[:, t, :, inner, :], load_sem.at[i]
            )
        )
        loads[i].start()
    smalls = [
        pltpu.make_async_copy(shifts_hbm, shifts_ref, small_sem.at[1]),
        pltpu.make_async_copy(fractions_hbm, fractions_ref, small_sem.at[2]),
    ]
    for copy in smalls:
        copy.start()

    barrier = pltpu.get_barrier_semaphore()
    peer = me + 2 * core - 1
    has_peer = (peer >= 0) & (peer < n)
    near = [device(level, side, 1 - core), device(level, 1 - side, core)]
    near += [device(at_level(o), side, core) for o in range(1, levels)]
    for where in near:
        pl.semaphore_signal(barrier, inc=1, device_id=where, device_id_type=MESH)

    @pl.when(has_peer)
    def _():
        pl.semaphore_signal(barrier, inc=1, device_id={"date": peer}, device_id_type=MESH)

    has_low = strip > 0
    has_high = strip < strips - 1

    @pl.when(has_low)
    def _():
        pl.semaphore_signal(barrier, inc=1, device_id={"strip": strip - 1}, device_id_type=MESH)

    @pl.when(has_high)
    def _():
        pl.semaphore_signal(barrier, inc=1, device_id={"strip": strip + 1}, device_id_type=MESH)

    edge_zero = jnp.zeros((kept, tiles, 2, HALO, frame.shape[4]), bf16)

    @pl.when(strip == 0)
    def _():
        frame[:, :, :, 0:HALO, :] = edge_zero

    @pl.when(strip == strips - 1)
    def _():
        frame[:, :, :, HALO + cols : 2 * HALO + cols, :] = edge_zero

    lane = lax.broadcasted_iota(jnp.int32, (GROUP, LANES), 1)

    def wide(count):
        return lax.broadcasted_iota(jnp.int32, (count, LANES), 1)

    def half(y):
        return pl.ds(y * half_units, half_units)

    used = chips * chip_units
    spare = cand.shape[1] - used
    if spare:
        for t in range(tiles):
            cand[t, used:] = jnp.zeros((spare, PACK, LANES), bf16)

    def move(depth, start, c):
        source = lax.broadcasted_iota(jnp.int32, (depth, LANES), 0)
        target = lax.broadcasted_iota(jnp.int32, (depth, LANES), 1)
        mine = (target < CHIP_SIZE) if c == 0 else (target >= CHIP_SIZE)
        hit = mine & (source == target - c * CHIP_SIZE + start)
        return jnp.where(hit, 1.0, 0.0).astype(bf16)

    even = [move(LANES, MARGIN, c) for c in range(2)]
    odd = [move(BAND, MARGIN + CHIP_SIZE, c) for c in range(2)]

    def pick(t):
        dates_row = dates_ref[0:1, :]
        date_lane = lax.broadcasted_iota(jnp.int32, (1, tiles), 1)
        date = jnp.sum(jnp.where(date_lane == t, dates_row, 0), axis=1, keepdims=True)
        gains = [
            jnp.broadcast_to(jnp.where(date == me * kept + d, 1.0, 0.0), (cols, frame.shape[4]))
            .astype(bf16)
            for d in range(kept)
        ]
        parts = []
        for c in range(2):
            total = frame[0, t, c, inner, :] * gains[0]
            for d in range(1, kept):
                total = total + frame[d, t, c, inner, :] * gains[d]
            parts.append(total)
        for a in range(chips_az):
            start = (a // 2) * LANES
            depth = min(BAND if a % 2 else LANES, frame.shape[4] - start)
            mixed = sum(
                jnp.dot(
                    parts[c][:, start : start + depth],
                    (odd if a % 2 else even)[c][:depth],
                    preferred_element_type=f32,
                )
                for c in range(2)
            ).astype(bf16)
            for r in range(chips_rg):
                unit = (r * chips_az + a) * chip_units
                cand[t, unit : unit + chip_units] = mixed[
                    r * CHIP_SIZE : (r + 1) * CHIP_SIZE
                ].reshape(chip_units, PACK, LANES)

    dates_copy.wait()
    loads[0].wait()
    pick(1 - core)

    beside = jnp.minimum(strip, 1) + jnp.minimum(strips - 1 - strip, 1)
    linked = jnp.where(has_peer, 1, 0)
    pl.semaphore_wait(barrier, len(near) + linked + beside)

    core_rs = [
        remote(cand.at[1 - core, span], core_in.at[span], core_send.at[0], core_recv.at[i],
               device(level, side, 1 - core))
        for i, span in enumerate((half(1 - side), tail, half(side)))
    ]
    for copy in core_rs:
        copy.start()

    order = ((core, core), (1 - core, 1 - core), (core, 1 - core), (1 - core, core))
    edges = []
    for i, (d, t) in enumerate(order):
        up = remote(
            frame_hbm.at[d, t, :, pl.ds(cols - HALO, HALO), :], frame.at[d, t, :, pl.ds(0, HALO), :],
            edge_send.at[0], edge_recv.at[0, i], {"strip": strip + 1},
        )
        down = remote(
            frame_hbm.at[d, t, :, pl.ds(0, HALO), :], frame.at[d, t, :, pl.ds(HALO + cols, HALO), :],
            edge_send.at[1], edge_recv.at[1, i], {"strip": strip - 1},
        )
        edges.append((up, down))

        @pl.when(has_high)
        def _():
            up.start()

        @pl.when(has_low)
        def _():
            down.start()

    def edge_wait(i):
        @pl.when(has_low)
        def _():
            edges[i][0].wait_recv()

        @pl.when(has_high)
        def _():
            edges[i][1].wait_recv()

    loads[1].wait()
    pick(core)

    def level_piece(y, z):
        return pl.ds(y * half_units + z * piece, piece)

    y_rs = [
        remote(y_out.at[level_piece(0, at_level(o))], y_in.at[k], y_send.at[0], side_recv.at[k],
               device(level, 1 - side, core))
        for k, o in enumerate(steps + [0])
    ]
    z_rs = [
        remote(z_out.at[k], z_in.at[k], z_send.at[0], z_recv.at[0],
               device(at_level(o), side, core))
        for k, o in enumerate(steps)
    ]
    mine = whole.at[core, level_piece(side, level)]
    z_ag = [
        remote(mine, mine, z_send.at[1], back_recv.at[k], device(at_level(o), side, core))
        for k, o in enumerate(steps)
    ]
    y_ag = []
    for k, o in enumerate(steps + [0]):
        part = whole.at[core, level_piece(side, at_level(levels - o))]
        y_ag.append(
            remote(part, part, y_send.at[1], y_recv.at[1], device(level, 1 - side, core))
        )
    core_ag = [
        remote(whole.at[core, span], whole.at[core, span], core_send.at[1], core_recv.at[3 + i],
               device(level, side, 1 - core))
        for i, span in enumerate((half(side), half(1 - side), tail))
    ]

    def tail_piece(z):
        return pl.ds(SIDES * half_units + z * strip_piece, strip_piece)

    tail_rs = [
        remote(across_out.at[pl.ds(at_level(o) * strip_piece, strip_piece)], across_in.at[k],
               z_send.at[2], z_recv.at[2], device(at_level(o), side, core))
        for k, o in enumerate(steps)
    ]
    tail_y = remote(over, over_in, y_send.at[2], y_recv.at[2], device(level, 1 - side, core))
    tail_mine = whole.at[core, tail_piece(level)]
    tail_ag = [
        remote(tail_mine, tail_mine, z_send.at[3], z_recv.at[3], device(at_level(o), side, core))
        for o in steps
    ]

    def all_of(ref, send, recv):
        return remote(ref, ref, send, recv, device(level, side, core))

    def tail_core():
        core_rs[1].wait_recv()
        across_out[...] = cand[core, tail] + core_in[tail]
        for copy in tail_rs:
            copy.start()

    def tail_side():
        all_of(across_in, z_send.at[2], z_recv.at[2]).wait_recv()
        total = across_out[pl.ds(level * strip_piece, strip_piece)]
        for k in range(len(steps)):
            total = total + across_in[k]
        over[...] = total
        tail_y.start()

    def tail_level():
        tail_y.wait_recv()
        whole[core, tail_piece(level)] = over[...] + over_in[...]
        for copy in tail_ag:
            copy.start()

    def tail_back():
        all_of(across_in, z_send.at[3], z_recv.at[3]).wait_recv()
        core_ag[2].start()

    def ref_core():
        core_rs[0].wait_recv()
        y_out[...] = cand[core, half(1 - side)] + core_in[half(1 - side)]
        for copy in y_rs:
            copy.start()

    def piece_sum(k, o):
        at = level_piece(side, at_level(o))
        y_rs[k].wait_recv()
        return cand[core, at] + core_in[at] + y_in[k]

    def ref_side(k):
        if k == 0:
            core_rs[2].wait_recv()
        z_out[k] = piece_sum(k, steps[k])
        z_rs[k].start()

    def ref_level():
        total = piece_sum(len(steps), 0)
        all_of(z_in, z_send.at[0], z_recv.at[0]).wait_recv()
        for k in range(len(steps)):
            total = total + z_in[k]
        whole[core, level_piece(side, level)] = total
        for copy in z_ag:
            copy.start()
        y_ag[len(steps)].start()

    def ref_back(k):
        z_ag[k].wait_recv()
        y_ag[k].start()
        if k == len(steps) - 1:
            core_ag[0].start()

    def ref_other():
        all_of(y_out, y_send.at[1], y_recv.at[1]).wait_recv()
        core_ag[1].start()

    ref_core()
    tail_core()

    smalls[0].wait()
    smalls[1].wait()

    for d in range(kept):
        for a in range(chips_az):
            row = (d * chips_az + a) * tiles
            for i in range(2):
                spots[i, row : row + tiles, :chips_rg] = shifts_ref[i, d, a]
                spots[2 + i, row : row + tiles, :chips_rg] = fractions_ref[i, d, a]
    spot_rows = kept * chips_az * tiles
    first_tap = MARGIN - TAP_COUNT // 2 + 1
    at = wide(spot_rows)
    for r in range(chips_rg):
        values = [
            jnp.broadcast_to(spots[i, 0:spot_rows, r : r + 1], (spot_rows, LANES)) for i in range(4)
        ]
        line_tap = ((LANES - at) & (LANES - 1)) - (values[0] + first_tap)
        line_base[r, 0:spot_rows, :] = tap_weights(line_tap, values[2])
        col_tap = at - (values[1] + (first_tap + HALO - MARGIN))
        col_base[r, 0:spot_rows, :] = tap_weights(col_tap, values[3])

    low_lane = wide(CHIP_SIZE) < CHIP_SIZE

    def halves(count):
        return wide(count) < CHIP_SIZE

    def chip_column(d, t, r, slot):
        row0 = r * CHIP_SIZE
        window = pl.ds(row0, WINDOW)

        def base(ref, a):
            return ref[r, pl.ds((d * chips_az + a) * tiles + t, 1), :]

        partial = [None] * chips_az
        reach = CHIP_SIZE + 2 * MARGIN
        for a in range(0, chips_az - 1, 2):
            b = a // 2
            span = slice(b * LANES, b * LANES + BAND)
            image = jnp.concatenate([frame[d, t, c, window, span] for c in range(2)], axis=0)
            first = spread(base(line_base, a), reach, 0)
            second = spread(base(line_base, a + 1), BAND - CHIP_SIZE, CHIP_SIZE)
            shared = reach - CHIP_SIZE
            matrix = jnp.concatenate(
                [
                    jnp.where(halves(CHIP_SIZE), first[:CHIP_SIZE], 0.0),
                    jnp.where(halves(shared), first[CHIP_SIZE:], second[:shared]),
                    jnp.where(halves(BAND - reach), 0.0, second[shared:]),
                ],
                axis=0,
            ).astype(bf16)
            out = jnp.dot(image, matrix, preferred_element_type=f32)
            re, im = out[:WINDOW], out[WINDOW:]
            left = halves(WINDOW)
            partial[a] = jnp.where(left, re, pltpu.roll(im, CHIP_SIZE, 1)).astype(bf16)
            partial[a + 1] = jnp.where(left, pltpu.roll(re, CHIP_SIZE, 1), im).astype(bf16)
        if chips_az % 2:
            a = chips_az - 1
            span = slice(a * CHIP_SIZE, a * CHIP_SIZE + reach)
            row = base(line_base, a)
            left = halves(reach)
            top = jnp.where(left, spread(row, reach, 0), 0.0).astype(bf16)
            bottom = jnp.where(left, 0.0, spread(row, reach, CHIP_SIZE)).astype(bf16)
            partial[a] = (
                jnp.dot(frame[d, t, 0, window, span], top, preferred_element_type=f32)
                + jnp.dot(frame[d, t, 1, window, span], bottom, preferred_element_type=f32)
            ).astype(bf16)
        for a in range(chips_az):
            matrix = spread(base(col_base, a), CHIP_SIZE, 0)[:, :WINDOW].astype(bf16)
            out = jnp.dot(matrix, partial[a], preferred_element_type=f32).astype(bf16)
            if slot is not None:
                unit = (r * chips_az + a) * chip_units
                sent[slot, pl.ds(unit, chip_units)] = out.reshape(chip_units, PACK, LANES)
            out = out.astype(f32)
            series[t, d + t, a, pl.ds(row0, CHIP_SIZE), :] = out
            power = jnp.sum((out * out).reshape(GROUP, GROUP, LANES), axis=0)
            totals[1 + 2 * kept + d, r, pl.ds((a * tiles + t) * GROUP, GROUP), :] = power

    def resample(i, first, last):
        d, t = order[i]

        for j in range(first, last):
            chip_column(d, t, (j + 1) % chips_rg, i if i < 2 else None)

    inside_cols = chips_rg - 2
    column = chips_az * chip_units
    outward = []
    for r in range(chips_rg):
        span = pl.ds(r * column, column)
        outward.append(
            remote(sent.at[0, span], got.at[0, span], next_send.at[0], next_recv.at[0], {"date": peer})
        )

    def outward_start(first, last):
        @pl.when(has_peer)
        def _():
            for r in range(first, last):
                outward[r].start()

    def outward_all():
        return remote(sent.at[0], got.at[0], next_send.at[0], next_recv.at[0], {"date": peer})

    inward = remote(
        sent.at[1], got.at[1], next_send.at[1], next_recv.at[1], device(level, side, 1 - core)
    )

    resample(0, 0, inside_cols)
    ref_side(0)
    edge_wait(0)
    resample(0, inside_cols, chips_rg)
    ref_side(1)
    resample(1, 0, inside_cols)
    for k in range(2, len(steps)):
        ref_side(k)
    outward_start(0, EARLY)
    edge_wait(1)
    resample(1, inside_cols, chips_rg)
    inward.start()
    tail_side()
    outward_start(EARLY, chips_rg)
    resample(2, 0, inside_cols)
    edge_wait(2)
    resample(2, inside_cols, chips_rg)
    edge_wait(3)
    resample(3, 0, chips_rg)

    looks_rg = cols // LOOK_RG
    look_rows = rows // LOOK_AZ

    def pick_rows(t, pos, a, s):
        return series[t, pos, a, pl.ds(s, looks_rg, stride=LOOK_RG), :]

    def look(t, early, wanted):
        for a in range(chips_az):
            sums = [jnp.zeros((looks_rg, LANES), f32) for _ in range(2 + len(wanted))]
            for s in range(LOOK_RG):
                first = pick_rows(t, early, a, s)
                second = pick_rows(t, early + 1, a, s)
                sums[0] = sums[0] + first * second
                sums[1] = sums[1] + first * pltpu.roll(second, CHIP_SIZE, 1)
                for i, pos in enumerate(wanted):
                    value = pick_rows(t, pos, a, s)
                    sums[2 + i] = sums[2 + i] + value * value
            span = slice(a * LANES, (a + 1) * LANES)
            row = pl.multiple_of((early * tiles + t) * looks_rg, GROUP)
            for c in range(2):
                cross_sums[c, pl.ds(row, looks_rg), span] = sums[c]
            for i, pos in enumerate(wanted):
                row = pl.multiple_of((pos * tiles + t) * looks_rg, GROUP)
                powers[pl.ds(row, looks_rg), span] = sums[2 + i]

    def unpack(i, t, pos):
        def body(j, carry):
            for a in range(chips_az):
                unit = (j * chips_az + a) * chip_units
                value = got[i, pl.ds(unit, chip_units)].reshape(CHIP_SIZE, LANES)
                row = pl.multiple_of(j * CHIP_SIZE, CHIP_SIZE)
                series[t, pos, a, pl.ds(row, CHIP_SIZE), :] = value.astype(f32)
            return carry

        lax.fori_loop(0, chips_rg, body, 0)

    look(1 - core, 1 - core, (1 - core, 2 - core))

    def build_selectors(a, carry):
        line = lax.broadcasted_iota(jnp.int32, (LANES, LANES), 0)
        y = lax.broadcasted_iota(jnp.int32, (LANES, LANES), 1)
        gap = a * CHIP_SIZE + (line & (CHIP_SIZE - 1)) - LOOK_AZ * y
        hit = (gap >= 0) & (gap < LOOK_AZ)
        span = pl.ds(pl.multiple_of(a * LANES, LANES), LANES)
        selectors[0, span, :] = jnp.where(hit, 1.0, 0.0).astype(bf16)
        selectors[1, span, :] = jnp.where(
            hit, jnp.where(line < CHIP_SIZE, -1.0, 1.0), 0.0
        ).astype(bf16)
        return carry

    lax.fori_loop(0, chips_az, build_selectors, 0)

    def correlate(t, first, count):
        for j in range(count):
            chip = first + j
            a = chip % chips_az
            r = chip // chips_az
            row = pl.multiple_of(r * CHIP_SIZE, CHIP_SIZE)
            to = pl.ds(pl.multiple_of((a * tiles + t) * GROUP, GROUP), GROUP)
            sums = [None] * (1 + 2 * kept)
            for g in range(chip_units):
                ref = whole[t, chip * chip_units + g].astype(f32)
                turned = pltpu.roll(ref, CHIP_SIZE, 1)
                terms = [ref * ref]
                for d in range(kept):
                    value = series[t, d + t, a, pl.ds(row + g * PACK, PACK), :]
                    terms += [ref * value, turned * value]
                for k, term in enumerate(terms):
                    term = term[:GROUP] + term[GROUP:]
                    sums[k] = term if sums[k] is None else sums[k] + term
            for k, value in enumerate(sums):
                totals[k, r, to, :] = value

    ref_level()
    tail_level()
    look(core, core, (core, 1 + core))
    inward.wait_recv()
    unpack(1, core, 2 * (1 - core))
    look(core, 1 - core, (2 * (1 - core),))

    @pl.when(has_peer)
    def _():
        outward_all().wait_recv()
        unpack(0, 1 - core, 2 * core)

    @pl.when(jnp.logical_not(has_peer))
    def _():
        series[1 - core, 2 * core] = jnp.zeros(series.shape[2:], f32)

    look(1 - core, core, (2 * core,))

    summed = [split_dot(cross_sums[c], selectors[c]) for c in range(2)]
    power = split_dot(powers[...], selectors[0])
    count = kept * tiles * looks_rg
    skip = tiles * looks_rg
    scale = jnp.sqrt((power[:count] + epsilon) * (power[skip : skip + count] + epsilon))
    coherence = jnp.concatenate([v / scale for v in summed], axis=0).T
    share = look_rows // n
    for j in range(n):
        out_buf[j] = coherence[j * share : (j + 1) * share]
    coh_in[me] = out_buf[me]
    for o in range(1, n):
        to = lax.rem(me + o, n)
        copy = remote(
            out_buf.at[to], coh_in.at[me], coh_send.at[0], coh_recv.at[0], {"date": to}
        )
        copy.start()

    for k in range(len(steps)):
        ref_back(k)
    tail_back()
    tail_chips = chips - tail_first
    correlate(core, side * half_chips, half_chips)
    correlate(core, tail_first, tail_chips)
    core_ag[0].wait_recv()
    correlate(1 - core, side * half_chips, half_chips)
    core_ag[2].wait_recv()
    correlate(1 - core, tail_first, tail_chips)
    ref_other()
    correlate(core, (1 - side) * half_chips, half_chips)
    core_ag[1].wait_recv()
    correlate(1 - core, (1 - side) * half_chips, half_chips)

    kinds = totals.shape[0]
    group_rows = totals.shape[2] // GROUP
    lane16 = wide(group_rows)
    sign = jnp.where(lane16 < CHIP_SIZE, 1.0, -1.0).astype(f32)
    folded = []
    for k in range(kinds):
        line = []
        for r in range(chips_rg):
            total = None
            for s in range(GROUP):
                value = totals[k, r, pl.ds(s, group_rows, stride=GROUP), :]
                total = value if total is None else total + value
            if 1 <= k <= 2 * kept and k % 2 == 0:
                total = total * sign
            line.append(total)
        folded.append(jnp.concatenate(line, axis=1))
    folded = jnp.concatenate(folded, axis=0)
    depth = chips_rg * LANES
    source = lax.broadcasted_iota(jnp.int32, (depth, LANES), 0)
    target = lax.broadcasted_iota(jnp.int32, (depth, LANES), 1)
    gap = source - target * LANES
    gather = jnp.where((gap >= 0) & (gap < LANES), 1.0, 0.0).astype(bf16)
    sums = split_dot(folded, gather)
    sums = [sums[k * group_rows : (k + 1) * group_rows] for k in range(kinds)]
    for d in range(kept):
        scale = jnp.sqrt((sums[0] + epsilon) * (sums[1 + 2 * kept + d] + epsilon))
        for c in range(2):
            value = sums[1 + 2 * d + c] / scale
            for a in range(chips_az):
                corr_ref[c, d, a] = value[a * tiles : (a + 1) * tiles, :chips_rg]

    others = pl.ds(0, n - 1)
    relays = remote(
        out_buf.at[others], coh_in.at[others], coh_send.at[0], coh_recv.at[0], {"date": me}
    )
    relays.wait_recv()
    pairs = n * kept
    lane_n = wide(n)
    for y in range(share):
        value = coh_in[:, y, :]
        ordered[y, pl.ds(0, n, stride=2), :] = value
        ordered[y, pl.ds(1, n, stride=2), :] = pltpu.roll(value, LANES - tiles * looks_rg, 1)
    lane_p = wide(pairs)
    for y in range(share):
        first = (lane_p & (2 * looks_rg - 1)) < looks_rg
        value = jnp.where(first, ordered[y, 0:pairs, :], ordered[y, 1 : pairs + 1, :]).T
        for c in range(2):
            for t in range(tiles):
                row = c * kept * tiles * looks_rg + t * looks_rg
                coh_ref[c, t, y] = value[row : row + looks_rg, : pairs - 1]

    relays.wait_send()
    inward.wait_send()
    for ref, sem in (
        (cand.at[1 - core], core_send.at[0]),
        (whole.at[core], core_send.at[1]),
        (y_out, y_send.at[0]),
        (y_out, y_send.at[1]),
        (over, y_send.at[2]),
        (z_out, z_send.at[0]),
        (z_out, z_send.at[1]),
        (across_in, z_send.at[2]),
        (across_in, z_send.at[3]),
    ):
        all_of(ref, sem, sem).wait_send()

    @pl.when(has_peer)
    def _():
        outward_all().wait_send()

    rim = frame.at[:, :, :, 0:HALO, :]

    @pl.when(has_high)
    def _():
        all_of(rim, edge_send.at[0], edge_send.at[0]).wait_send()

    @pl.when(has_low)
    def _():
        all_of(rim, edge_send.at[1], edge_send.at[1]).wait_send()


def per_device(n, strips, acquisitions, shifts, fractions, ref_dates):
    kept, tiles, _, all_rows, cols = acquisitions.shape
    rows = all_rows - 2 * MARGIN
    chips_az, chips_rg = shifts.shape[3:]
    chips = chips_az * chips_rg
    units = chips * CHIP_SIZE // PACK
    levels = n // (CORES * SIDES)
    piece = max(units * SHARE // 100 // levels, 1)
    half_units = piece * levels
    strip_piece = -(-(units - SIDES * half_units) // levels)
    total_units = SIDES * half_units + levels * strip_piece
    looks_rg = cols // LOOK_RG
    look_rows = rows // LOOK_AZ
    share = look_rows // n
    spot_rows = -(-(kept * chips_az * tiles) // GROUP) * GROUP
    group_rows = -(-(chips_az * tiles) // GROUP) * GROUP
    kinds = 1 + 3 * kept
    f32 = jnp.float32
    bf16 = jnp.bfloat16
    dma = pltpu.SemaphoreType.DMA
    vmem = pl.BlockSpec(memory_space=pltpu.VMEM)
    frames = jnp.swapaxes(acquisitions, 3, 4)
    order = (0, 1, 3, 2, 4)
    coh, corr = pl.pallas_call(
        functools.partial(kernel, n, strips, (tiles, kept, chips_az, chips_rg, rows, cols)),
        out_shape=(
            jax.ShapeDtypeStruct((2, tiles, share, looks_rg, n * kept - 1), f32),
            jax.ShapeDtypeStruct((2, kept, chips_az, tiles, chips_rg), f32),
        ),
        in_specs=[pl.BlockSpec(memory_space=pltpu.HBM)] * 4,
        out_specs=(vmem, vmem),
        scratch_shapes=[
            pltpu.VMEM((kept, tiles, 2, cols + 2 * HALO, all_rows), bf16),
            pltpu.VMEM((2, kept, chips_az, tiles, chips_rg), jnp.int32),
            pltpu.VMEM((2, kept, chips_az, tiles, chips_rg), jnp.int32),
            pltpu.VMEM((1, tiles), jnp.int32),
            pltpu.VMEM((4, spot_rows, LANES), jnp.int32),
            pltpu.VMEM((chips_rg, spot_rows, LANES), f32),
            pltpu.VMEM((chips_rg, spot_rows, LANES), f32),
            pltpu.VMEM((tiles, total_units, PACK, LANES), bf16),
            pltpu.VMEM((total_units, PACK, LANES), bf16),
            pltpu.VMEM((half_units, PACK, LANES), bf16),
            pltpu.VMEM((levels, piece, PACK, LANES), bf16),
            pltpu.VMEM((levels - 1, piece, PACK, LANES), bf16),
            pltpu.VMEM((levels - 1, piece, PACK, LANES), bf16),
            pltpu.VMEM((levels * strip_piece, PACK, LANES), bf16),
            pltpu.VMEM((levels - 1, strip_piece, PACK, LANES), bf16),
            pltpu.VMEM((strip_piece, PACK, LANES), bf16),
            pltpu.VMEM((strip_piece, PACK, LANES), bf16),
            pltpu.VMEM((tiles, total_units, PACK, LANES), bf16),
            pltpu.VMEM((tiles, kept + 1, chips_az, cols, LANES), f32),
            pltpu.VMEM((2, units, PACK, LANES), bf16),
            pltpu.VMEM((2, units, PACK, LANES), bf16),
            pltpu.VMEM((2, kept * tiles * looks_rg, chips_az * LANES), f32),
            pltpu.VMEM(((kept + 1) * tiles * looks_rg, chips_az * LANES), f32),
            pltpu.VMEM((2, chips_az * LANES, LANES), bf16),
            pltpu.VMEM((n, share, LANES), f32),
            pltpu.VMEM((n, share, LANES), f32),
            pltpu.VMEM((share, n * kept + GROUP, LANES), f32),
            pltpu.VMEM((kinds, chips_rg, group_rows * GROUP, LANES), f32),
            dma((2,)), dma((3,)), dma((2,)), dma((2, 4)), dma((2,)), dma((6,)),
            dma((3,)), dma((3,)), dma((4,)), dma((4,)), dma((levels,)), dma((levels - 1,)),
            dma((2,)), dma((2,)), dma((1,)), dma((1,)),
        ],
        compiler_params=pltpu.CompilerParams(
            collective_id=0, has_side_effects=True, vmem_limit_bytes=50 * 1024 * 1024
        ),
    )(*[pltpu.with_memory_space_constraint(v, pltpu.HBM) for v in (frames, shifts.transpose(order), fractions.transpose(order), ref_dates[None])])
    return (corr.transpose(order), coh.transpose(0, 4, 1, 2, 3))


def solution(mesh):
    return jax.shard_map(
        functools.partial(per_device, mesh.shape["date"], mesh.shape["strip"]),
        mesh=mesh,
        in_specs=(
            P("date", None, None, None, "strip"),
            P(None, "date", None, None, "strip"),
            P(None, "date", None, None, "strip"),
            P(),
        ),
        out_specs=(P(None, "date", None, None, "strip"), P(None, None, None, "date", "strip")),
        check_vma=False,
    )
```

```python
import functools

import jax
import jax.numpy as jnp
from jax import lax
from jax.experimental import pallas as pl
from jax.experimental.pallas import tpu as pltpu
from jax.sharding import PartitionSpec as P

CHIP_SIZE = 64
TAP_COUNT = 8
SUBSTEPS = 64
LOOK_AZ = 5
LOOK_RG = 20
MARGIN = 12
LANES = 128
GROUP = 8
PACK = 16
HALO = 16
WINDOW = 96
BAND = 160
CORES = 2
SIDES = 2
EARLY = 2
SHARE = 28

epsilon = 1e-06
COS_TERMS = (1.0, -1 / 2, 1 / 24, -1 / 720, 1 / 40320, -1 / 3628800, 1 / 479001600, -1 / 87178291200)
MESH = pl.DeviceIdType.MESH


def half_turn_cos(square):
    total = jnp.full(square.shape, COS_TERMS[-1], jnp.float32)
    for term in COS_TERMS[-2::-1]:
        total = total * square + term
    return total


def tap_weights(k, fraction):
    part = fraction.astype(jnp.float32) / SUBSTEPS
    distance = k.astype(jnp.float32) - (TAP_COUNT // 2 - 1) - part
    turn = (part - 0.5) * jnp.pi
    sine = half_turn_cos(turn * turn)
    sine = jnp.where((k & 1) == 0, sine, -sine)
    sine = jnp.where(part == 0.0, 0.0, sine)
    angle = jnp.pi * distance
    sinc = jnp.where(distance == 0.0, 1.0, sine / jnp.where(distance == 0.0, 1.0, angle))
    eighth = distance * (jnp.pi / TAP_COUNT)
    window = half_turn_cos(eighth * eighth)
    weights = sinc * (window * window)
    weights = jnp.where((k >= 0) & (k < TAP_COUNT), weights, 0.0)
    return weights / jnp.sum(weights, axis=1, keepdims=True)


def spread(row, count, start):
    tall = jnp.broadcast_to(row, (count, LANES))
    return pltpu.roll(tall, start, 1, stride=1, stride_axis=0)


def split_dot(values, selector):
    high = values.astype(jnp.bfloat16)
    low = (values - high.astype(jnp.float32)).astype(jnp.bfloat16)
    return jnp.dot(high, selector, preferred_element_type=jnp.float32) + jnp.dot(
        low, selector, preferred_element_type=jnp.float32
    )


def kernel(
    n, strips, dims,
    frame_hbm, shifts_hbm, fractions_hbm, dates_hbm,
    coh_ref, corr_ref,
    frame, shifts_ref, fractions_ref, dates_ref, spots, line_base, col_base,
    cand, core_in, y_out, y_in, z_out, z_in, across_out, across_in, over, over_in, whole,
    series, sent, got, cross_sums, powers, selectors, out_buf, coh_in, ordered, totals, gather,
    load_sem, small_sem, edge_send, edge_recv, core_send, core_recv, y_send, y_recv,
    z_send, z_recv, side_recv, back_recv, next_send, next_recv, coh_send, coh_recv,
):
    tiles, kept, chips_az, chips_rg, rows, cols = dims
    me = lax.axis_index("date")
    strip = lax.axis_index("strip")
    core = me % CORES
    side = (me // CORES) % SIDES
    levels = n // (CORES * SIDES)
    level = me // (CORES * SIDES)
    bf16 = jnp.bfloat16
    f32 = jnp.float32
    chips = chips_az * chips_rg
    chip_units = CHIP_SIZE // PACK
    piece, strip_piece = y_in.shape[1], across_in.shape[1]
    half_units = levels * piece
    half_chips = half_units // chip_units
    tail_first = SIDES * half_chips
    tail = pl.ds(SIDES * half_units, levels * strip_piece)
    steps = [levels // 2] + [o for o in range(1, levels) if o != levels // 2]

    def at_level(o):
        return lax.rem(level + o, levels)

    def device(z, y, c):
        return {"date": (z * SIDES + y) * CORES + c}

    def remote(src, dst, send, recv, where):
        return pltpu.make_async_remote_copy(
            src_ref=src, dst_ref=dst, send_sem=send, recv_sem=recv,
            device_id=where, device_id_type=MESH,
        )

    inner = pl.ds(HALO, cols)
    group_rows = totals.shape[2] // (tiles * GROUP)
    dates_copy = pltpu.make_async_copy(dates_hbm, dates_ref, small_sem.at[0])
    dates_copy.start()
    loads = []
    for i, t in enumerate((1 - core, core)):
        loads.append(
            pltpu.make_async_copy(
                frame_hbm.at[:, t], frame.at[:, t, :, inner, :], load_sem.at[i]
            )
        )
        loads[i].start()
    smalls = [
        pltpu.make_async_copy(shifts_hbm, shifts_ref, small_sem.at[1]),
        pltpu.make_async_copy(fractions_hbm, fractions_ref, small_sem.at[2]),
    ]
    for copy in smalls:
        copy.start()

    barrier = pltpu.get_barrier_semaphore()
    peer = me + 2 * core - 1
    has_peer = (peer >= 0) & (peer < n)
    near = [device(level, side, 1 - core), device(level, 1 - side, core)]
    near += [device(at_level(o), side, core) for o in range(1, levels)]
    for where in near:
        pl.semaphore_signal(barrier, inc=1, device_id=where, device_id_type=MESH)

    @pl.when(has_peer)
    def _():
        pl.semaphore_signal(barrier, inc=1, device_id={"date": peer}, device_id_type=MESH)

    has_low = strip > 0
    has_high = strip < strips - 1

    @pl.when(has_low)
    def _():
        pl.semaphore_signal(barrier, inc=1, device_id={"strip": strip - 1}, device_id_type=MESH)

    @pl.when(has_high)
    def _():
        pl.semaphore_signal(barrier, inc=1, device_id={"strip": strip + 1}, device_id_type=MESH)

    edge_zero = jnp.zeros((kept, tiles, 2, HALO, frame.shape[4]), bf16)

    @pl.when(strip == 0)
    def _():
        frame[:, :, :, 0:HALO, :] = edge_zero

    @pl.when(strip == strips - 1)
    def _():
        frame[:, :, :, HALO + cols : 2 * HALO + cols, :] = edge_zero

    lane = lax.broadcasted_iota(jnp.int32, (GROUP, LANES), 1)

    def wide(count):
        return lax.broadcasted_iota(jnp.int32, (count, LANES), 1)

    def half(y):
        return pl.ds(y * half_units, half_units)

    used = chips * chip_units
    spare = cand.shape[1] - used
    if spare:
        for t in range(tiles):
            cand[t, used:] = jnp.zeros((spare, PACK, LANES), bf16)

    def move(depth, start, c):
        source = lax.broadcasted_iota(jnp.int32, (depth, LANES), 0)
        target = lax.broadcasted_iota(jnp.int32, (depth, LANES), 1)
        mine = (target < CHIP_SIZE) if c == 0 else (target >= CHIP_SIZE)
        hit = mine & (source == target - c * CHIP_SIZE + start)
        return jnp.where(hit, 1.0, 0.0).astype(bf16)

    even = [move(LANES, MARGIN, c) for c in range(2)]
    odd = [move(BAND, MARGIN + CHIP_SIZE, c) for c in range(2)]

    def pick(t):
        dates_row = dates_ref[0:1, :]
        date_lane = lax.broadcasted_iota(jnp.int32, (1, tiles), 1)
        date = jnp.sum(jnp.where(date_lane == t, dates_row, 0), axis=1, keepdims=True)
        gains = [
            jnp.broadcast_to(jnp.where(date == me * kept + d, 1.0, 0.0), (cols, frame.shape[4]))
            .astype(bf16)
            for d in range(kept)
        ]
        parts = []
        for c in range(2):
            total = frame[0, t, c, inner, :] * gains[0]
            for d in range(1, kept):
                total = total + frame[d, t, c, inner, :] * gains[d]
            parts.append(total)
        for a in range(chips_az):
            start = (a // 2) * LANES
            depth = min(BAND if a % 2 else LANES, frame.shape[4] - start)
            mixed = sum(
                jnp.dot(
                    parts[c][:, start : start + depth],
                    (odd if a % 2 else even)[c][:depth],
                    preferred_element_type=f32,
                )
                for c in range(2)
            ).astype(bf16)
            for r in range(chips_rg):
                unit = (r * chips_az + a) * chip_units
                cand[t, unit : unit + chip_units] = mixed[
                    r * CHIP_SIZE : (r + 1) * CHIP_SIZE
                ].reshape(chip_units, PACK, LANES)

    dates_copy.wait()
    loads[0].wait()
    pick(1 - core)

    beside = jnp.minimum(strip, 1) + jnp.minimum(strips - 1 - strip, 1)
    linked = jnp.where(has_peer, 1, 0)
    pl.semaphore_wait(barrier, len(near) + linked + beside)

    core_rs = [
        remote(cand.at[1 - core, span], core_in.at[span], core_send.at[0], core_recv.at[i],
               device(level, side, 1 - core))
        for i, span in enumerate((half(1 - side), tail, half(side)))
    ]
    for copy in core_rs:
        copy.start()

    order = ((core, core), (1 - core, 1 - core), (core, 1 - core), (1 - core, core))
    edges = []
    for i, (d, t) in enumerate(order):
        up = remote(
            frame_hbm.at[d, t, :, pl.ds(cols - HALO, HALO), :], frame.at[d, t, :, pl.ds(0, HALO), :],
            edge_send.at[0], edge_recv.at[0, i], {"strip": strip + 1},
        )
        down = remote(
            frame_hbm.at[d, t, :, pl.ds(0, HALO), :], frame.at[d, t, :, pl.ds(HALO + cols, HALO), :],
            edge_send.at[1], edge_recv.at[1, i], {"strip": strip - 1},
        )
        edges.append((up, down))

        @pl.when(has_high)
        def _():
            up.start()

        @pl.when(has_low)
        def _():
            down.start()

    def edge_wait(i):
        @pl.when(has_low)
        def _():
            edges[i][0].wait_recv()

        @pl.when(has_high)
        def _():
            edges[i][1].wait_recv()

    loads[1].wait()
    pick(core)

    def level_piece(y, z):
        return pl.ds(y * half_units + z * piece, piece)

    y_rs = [
        remote(y_out.at[level_piece(0, at_level(o))], y_in.at[k], y_send.at[0], side_recv.at[k],
               device(level, 1 - side, core))
        for k, o in enumerate(steps + [0])
    ]
    z_rs = [
        remote(z_out.at[k], z_in.at[k], z_send.at[0], z_recv.at[0],
               device(at_level(o), side, core))
        for k, o in enumerate(steps)
    ]
    mine = whole.at[core, level_piece(side, level)]
    z_ag = [
        remote(mine, mine, z_send.at[1], back_recv.at[k], device(at_level(o), side, core))
        for k, o in enumerate(steps)
    ]
    y_ag = []
    for k, o in enumerate(steps + [0]):
        part = whole.at[core, level_piece(side, at_level(levels - o))]
        y_ag.append(
            remote(part, part, y_send.at[1], y_recv.at[1], device(level, 1 - side, core))
        )
    core_ag = [
        remote(whole.at[core, span], whole.at[core, span], core_send.at[1], core_recv.at[3 + i],
               device(level, side, 1 - core))
        for i, span in enumerate((half(side), half(1 - side), tail))
    ]

    def tail_piece(z):
        return pl.ds(SIDES * half_units + z * strip_piece, strip_piece)

    tail_rs = [
        remote(across_out.at[pl.ds(at_level(o) * strip_piece, strip_piece)], across_in.at[k],
               z_send.at[2], z_recv.at[2], device(at_level(o), side, core))
        for k, o in enumerate(steps)
    ]
    tail_y = remote(over, over_in, y_send.at[2], y_recv.at[2], device(level, 1 - side, core))
    tail_mine = whole.at[core, tail_piece(level)]
    tail_ag = [
        remote(tail_mine, tail_mine, z_send.at[3], z_recv.at[3], device(at_level(o), side, core))
        for o in steps
    ]

    def all_of(ref, send, recv):
        return remote(ref, ref, send, recv, device(level, side, core))

    def tail_core():
        core_rs[1].wait_recv()
        across_out[...] = cand[core, tail] + core_in[tail]
        for copy in tail_rs:
            copy.start()

    def tail_side():
        all_of(across_in, z_send.at[2], z_recv.at[2]).wait_recv()
        total = across_out[pl.ds(level * strip_piece, strip_piece)]
        for k in range(len(steps)):
            total = total + across_in[k]
        over[...] = total
        tail_y.start()

    def tail_level():
        tail_y.wait_recv()
        whole[core, tail_piece(level)] = over[...] + over_in[...]
        for copy in tail_ag:
            copy.start()

    def tail_back():
        all_of(across_in, z_send.at[3], z_recv.at[3]).wait_recv()
        core_ag[2].start()

    def ref_core():
        core_rs[0].wait_recv()
        y_out[...] = cand[core, half(1 - side)] + core_in[half(1 - side)]
        for copy in y_rs:
            copy.start()

    def piece_sum(k, o):
        at = level_piece(side, at_level(o))
        y_rs[k].wait_recv()
        return cand[core, at] + core_in[at] + y_in[k]

    def ref_side(k):
        if k == 0:
            core_rs[2].wait_recv()
        z_out[k] = piece_sum(k, steps[k])
        z_rs[k].start()

    def ref_level():
        total = piece_sum(len(steps), 0)
        all_of(z_in, z_send.at[0], z_recv.at[0]).wait_recv()
        for k in range(len(steps)):
            total = total + z_in[k]
        whole[core, level_piece(side, level)] = total
        for copy in z_ag:
            copy.start()
        y_ag[len(steps)].start()

    def ref_back(k):
        z_ag[k].wait_recv()
        y_ag[k].start()
        if k == len(steps) - 1:
            core_ag[0].start()

    def ref_other():
        all_of(y_out, y_send.at[1], y_recv.at[1]).wait_recv()
        core_ag[1].start()

    ref_core()
    tail_core()

    smalls[0].wait()
    smalls[1].wait()

    for d in range(kept):
        for a in range(chips_az):
            row = (d * chips_az + a) * tiles
            for i in range(2):
                spots[i, row : row + tiles, :chips_rg] = shifts_ref[i, d, a]
                spots[2 + i, row : row + tiles, :chips_rg] = fractions_ref[i, d, a]
    spot_rows = kept * chips_az * tiles
    first_tap = MARGIN - TAP_COUNT // 2 + 1
    at = wide(spot_rows)
    for r in range(chips_rg):
        values = [
            jnp.broadcast_to(spots[i, 0:spot_rows, r : r + 1], (spot_rows, LANES)) for i in range(4)
        ]
        line_tap = ((LANES - at) & (LANES - 1)) - (values[0] + first_tap)
        line_base[r, 0:spot_rows, :] = tap_weights(line_tap, values[2])
        col_tap = at - (values[1] + (first_tap + HALO - MARGIN))
        col_base[r, 0:spot_rows, :] = tap_weights(col_tap, values[3])

    low_lane = wide(CHIP_SIZE) < CHIP_SIZE

    def halves(count):
        return wide(count) < CHIP_SIZE

    def chip_column(d, t, r, slot):
        row0 = r * CHIP_SIZE
        window = pl.ds(row0, WINDOW)

        def base(ref, a):
            return ref[r, pl.ds((d * chips_az + a) * tiles + t, 1), :]

        partial = [None] * chips_az
        reach = CHIP_SIZE + 2 * MARGIN
        for a in range(0, chips_az - 1, 2):
            b = a // 2
            span = slice(b * LANES, b * LANES + BAND)
            image = jnp.concatenate([frame[d, t, c, window, span] for c in range(2)], axis=0)
            first = spread(base(line_base, a), reach, 0)
            second = spread(base(line_base, a + 1), BAND - CHIP_SIZE, CHIP_SIZE)
            shared = reach - CHIP_SIZE
            matrix = jnp.concatenate(
                [
                    jnp.where(halves(CHIP_SIZE), first[:CHIP_SIZE], 0.0),
                    jnp.where(halves(shared), first[CHIP_SIZE:], second[:shared]),
                    jnp.where(halves(BAND - reach), 0.0, second[shared:]),
                ],
                axis=0,
            ).astype(bf16)
            out = jnp.dot(image, matrix, preferred_element_type=f32)
            re, im = out[:WINDOW], out[WINDOW:]
            left = halves(WINDOW)
            partial[a] = jnp.where(left, re, pltpu.roll(im, CHIP_SIZE, 1)).astype(bf16)
            partial[a + 1] = jnp.where(left, pltpu.roll(re, CHIP_SIZE, 1), im).astype(bf16)
        if chips_az % 2:
            a = chips_az - 1
            span = slice(a * CHIP_SIZE, a * CHIP_SIZE + reach)
            row = base(line_base, a)
            left = halves(reach)
            top = jnp.where(left, spread(row, reach, 0), 0.0).astype(bf16)
            bottom = jnp.where(left, 0.0, spread(row, reach, CHIP_SIZE)).astype(bf16)
            partial[a] = (
                jnp.dot(frame[d, t, 0, window, span], top, preferred_element_type=f32)
                + jnp.dot(frame[d, t, 1, window, span], bottom, preferred_element_type=f32)
            ).astype(bf16)
        for a in range(chips_az):
            matrix = spread(base(col_base, a), CHIP_SIZE, 0)[:, :WINDOW].astype(bf16)
            out = jnp.dot(matrix, partial[a], preferred_element_type=f32).astype(bf16)
            if slot is not None:
                unit = (r * chips_az + a) * chip_units
                sent[slot, pl.ds(unit, chip_units)] = out.reshape(chip_units, PACK, LANES)
            out = out.astype(f32)
            series[t, d + t, a, pl.ds(row0, CHIP_SIZE), :] = out
            power = jnp.sum((out * out).reshape(GROUP, GROUP, LANES), axis=0)
            totals[1 + 2 * kept + d, r, pl.ds((t * group_rows + a) * GROUP, GROUP), :] = power

    def resample(i, first, last):
        d, t = order[i]

        for j in range(first, last):
            chip_column(d, t, (j + 1) % chips_rg, i if i < 2 else None)

    inside_cols = chips_rg - 2
    column = chips_az * chip_units
    outward = []
    for r in range(chips_rg):
        span = pl.ds(r * column, column)
        outward.append(
            remote(sent.at[0, span], got.at[0, span], next_send.at[0], next_recv.at[0], {"date": peer})
        )

    def outward_start(first, last):
        @pl.when(has_peer)
        def _():
            for r in range(first, last):
                outward[r].start()

    def outward_all():
        return remote(sent.at[0], got.at[0], next_send.at[0], next_recv.at[0], {"date": peer})

    inward = remote(
        sent.at[1], got.at[1], next_send.at[1], next_recv.at[1], device(level, side, 1 - core)
    )

    resample(0, 0, inside_cols)
    ref_side(0)
    edge_wait(0)
    resample(0, inside_cols, chips_rg)
    ref_side(1)
    resample(1, 0, inside_cols)
    for k in range(2, len(steps)):
        ref_side(k)
    outward_start(0, EARLY)
    edge_wait(1)
    resample(1, inside_cols, chips_rg)
    inward.start()
    tail_side()
    outward_start(EARLY, chips_rg)
    resample(2, 0, inside_cols)
    edge_wait(2)
    resample(2, inside_cols, chips_rg)
    ref_level()
    resample(3, 0, inside_cols)
    edge_wait(3)
    resample(3, inside_cols, chips_rg)

    looks_rg = cols // LOOK_RG
    look_rows = rows // LOOK_AZ

    def pick_rows(t, pos, a, s):
        return series[t, pos, a, pl.ds(s, looks_rg, stride=LOOK_RG), :]

    def look(t, early, wanted):
        for a in range(chips_az):
            sums = [jnp.zeros((looks_rg, LANES), f32) for _ in range(2 + len(wanted))]
            for s in range(LOOK_RG):
                first = pick_rows(t, early, a, s)
                second = pick_rows(t, early + 1, a, s)
                sums[0] = sums[0] + first * second
                sums[1] = sums[1] + first * pltpu.roll(second, CHIP_SIZE, 1)
                for i, pos in enumerate(wanted):
                    value = pick_rows(t, pos, a, s)
                    sums[2 + i] = sums[2 + i] + value * value
            span = slice(a * LANES, (a + 1) * LANES)
            row = pl.multiple_of((early * tiles + t) * looks_rg, GROUP)
            for c in range(2):
                cross_sums[c, pl.ds(row, looks_rg), span] = sums[c]
            for i, pos in enumerate(wanted):
                row = pl.multiple_of((pos * tiles + t) * looks_rg, GROUP)
                powers[pl.ds(row, looks_rg), span] = sums[2 + i]

    def unpack(i, t, pos):
        def body(j, carry):
            for a in range(chips_az):
                unit = (j * chips_az + a) * chip_units
                value = got[i, pl.ds(unit, chip_units)].reshape(CHIP_SIZE, LANES)
                row = pl.multiple_of(j * CHIP_SIZE, CHIP_SIZE)
                series[t, pos, a, pl.ds(row, CHIP_SIZE), :] = value.astype(f32)
            return carry

        lax.fori_loop(0, chips_rg, body, 0)

    look(1 - core, 1 - core, (1 - core, 2 - core))

    def build_selectors(a, carry):
        line = lax.broadcasted_iota(jnp.int32, (LANES, LANES), 0)
        y = lax.broadcasted_iota(jnp.int32, (LANES, LANES), 1)
        gap = a * CHIP_SIZE + (line & (CHIP_SIZE - 1)) - LOOK_AZ * y
        hit = (gap >= 0) & (gap < LOOK_AZ)
        span = pl.ds(pl.multiple_of(a * LANES, LANES), LANES)
        selectors[0, span, :] = jnp.where(hit, 1.0, 0.0).astype(bf16)
        selectors[1, span, :] = jnp.where(
            hit, jnp.where(line < CHIP_SIZE, -1.0, 1.0), 0.0
        ).astype(bf16)
        return carry

    lax.fori_loop(0, chips_az, build_selectors, 0)
    source = lax.broadcasted_iota(jnp.int32, gather.shape, 0)
    target = lax.broadcasted_iota(jnp.int32, gather.shape, 1)
    gap = source - target * LANES
    gather[...] = jnp.where((gap >= 0) & (gap < LANES), 1.0, 0.0).astype(bf16)

    def correlate(t, first, count):
        for j in range(count):
            chip = first + j
            a = chip % chips_az
            r = chip // chips_az
            row = pl.multiple_of(r * CHIP_SIZE, CHIP_SIZE)
            to = pl.ds(pl.multiple_of((t * group_rows + a) * GROUP, GROUP), GROUP)
            sums = [None] * (1 + 2 * kept)
            for g in range(chip_units):
                ref = whole[t, chip * chip_units + g].astype(f32)
                turned = pltpu.roll(ref, CHIP_SIZE, 1)
                terms = [ref * ref]
                for d in range(kept):
                    value = series[t, d + t, a, pl.ds(row + g * PACK, PACK), :]
                    terms += [ref * value, turned * value]
                for k, term in enumerate(terms):
                    term = term[:GROUP] + term[GROUP:]
                    sums[k] = term if sums[k] is None else sums[k] + term
            for k, value in enumerate(sums):
                totals[k, r, to, :] = value

    look(core, core, (core, 1 + core))
    inward.wait_recv()
    unpack(1, core, 2 * (1 - core))
    look(core, 1 - core, (2 * (1 - core),))

    for k in range(2):
        ref_back(k)
    tail_level()

    @pl.when(has_peer)
    def _():
        outward_all().wait_recv()
        unpack(0, 1 - core, 2 * core)

    @pl.when(jnp.logical_not(has_peer))
    def _():
        series[1 - core, 2 * core] = jnp.zeros(series.shape[2:], f32)

    look(1 - core, core, (2 * core,))

    summed = [split_dot(cross_sums[c], selectors[c]) for c in range(2)]
    power = split_dot(powers[...], selectors[0])
    count = kept * tiles * looks_rg
    skip = tiles * looks_rg
    scale = jnp.sqrt((power[:count] + epsilon) * (power[skip : skip + count] + epsilon))
    coherence = jnp.concatenate([v / scale for v in summed], axis=0).T
    share = look_rows // n
    for j in range(n):
        out_buf[j] = coherence[j * share : (j + 1) * share]
    coh_in[me] = out_buf[me]
    for o in range(1, n):
        to = lax.rem(me + o, n)
        copy = remote(
            out_buf.at[to], coh_in.at[me], coh_send.at[0], coh_recv.at[0], {"date": to}
        )
        copy.start()

    for k in range(2, len(steps)):
        ref_back(k)
    tail_back()
    tail_chips = chips - tail_first
    correlate(core, side * half_chips, half_chips)
    correlate(core, tail_first, tail_chips)
    core_ag[0].wait_recv()
    correlate(1 - core, side * half_chips, half_chips)
    core_ag[2].wait_recv()
    correlate(1 - core, tail_first, tail_chips)
    ref_other()
    kinds = totals.shape[0]

    def finish(t):
        sign = jnp.where(wide(group_rows) < CHIP_SIZE, 1.0, -1.0).astype(f32)
        folded = []
        for k in range(kinds):
            line = []
            for r in range(chips_rg):
                total = None
                for s in range(GROUP):
                    at = pl.ds(t * (group_rows * GROUP) + s, group_rows, stride=GROUP)
                    value = totals[k, r, at, :]
                    total = value if total is None else total + value
                if 1 <= k <= 2 * kept and k % 2 == 0:
                    total = total * sign
                line.append(total)
            folded.append(jnp.concatenate(line, axis=1))
        sums = split_dot(jnp.concatenate(folded, axis=0), gather[...])
        sums = [sums[k * group_rows : (k + 1) * group_rows] for k in range(kinds)]
        for d in range(kept):
            scale = jnp.sqrt((sums[0] + epsilon) * (sums[1 + 2 * kept + d] + epsilon))
            for c in range(2):
                value = sums[1 + 2 * d + c] / scale
                for a in range(chips_az):
                    corr_ref[c, d, a, pl.ds(t, 1), :] = value[a : a + 1, :chips_rg]

    correlate(core, (1 - side) * half_chips, half_chips)
    finish(core)

    others = pl.ds(0, n - 1)
    relays = remote(
        out_buf.at[others], coh_in.at[others], coh_send.at[0], coh_recv.at[0], {"date": me}
    )
    relays.wait_recv()
    pairs = n * kept
    lane_n = wide(n)
    for y in range(share):
        value = coh_in[:, y, :]
        ordered[y, pl.ds(0, n, stride=2), :] = value
        ordered[y, pl.ds(1, n, stride=2), :] = pltpu.roll(value, LANES - tiles * looks_rg, 1)
    lane_p = wide(pairs)
    for y in range(share):
        first = (lane_p & (2 * looks_rg - 1)) < looks_rg
        value = jnp.where(first, ordered[y, 0:pairs, :], ordered[y, 1 : pairs + 1, :]).T
        for c in range(2):
            for t in range(tiles):
                row = c * kept * tiles * looks_rg + t * looks_rg
                coh_ref[c, t, y] = value[row : row + looks_rg, : pairs - 1]

    core_ag[1].wait_recv()
    correlate(1 - core, (1 - side) * half_chips, half_chips)
    finish(1 - core)

    relays.wait_send()
    inward.wait_send()
    for ref, sem in (
        (cand.at[1 - core], core_send.at[0]),
        (whole.at[core], core_send.at[1]),
        (y_out, y_send.at[0]),
        (y_out, y_send.at[1]),
        (over, y_send.at[2]),
        (z_out, z_send.at[0]),
        (z_out, z_send.at[1]),
        (across_in, z_send.at[2]),
        (across_in, z_send.at[3]),
    ):
        all_of(ref, sem, sem).wait_send()

    @pl.when(has_peer)
    def _():
        outward_all().wait_send()

    rim = frame.at[:, :, :, 0:HALO, :]

    @pl.when(has_high)
    def _():
        all_of(rim, edge_send.at[0], edge_send.at[0]).wait_send()

    @pl.when(has_low)
    def _():
        all_of(rim, edge_send.at[1], edge_send.at[1]).wait_send()


def per_device(n, strips, acquisitions, shifts, fractions, ref_dates):
    kept, tiles, _, all_rows, cols = acquisitions.shape
    rows = all_rows - 2 * MARGIN
    chips_az, chips_rg = shifts.shape[3:]
    chips = chips_az * chips_rg
    units = chips * CHIP_SIZE // PACK
    levels = n // (CORES * SIDES)
    piece = max(units * SHARE // 100 // levels, 1)
    half_units = piece * levels
    strip_piece = -(-(units - SIDES * half_units) // levels)
    total_units = SIDES * half_units + levels * strip_piece
    looks_rg = cols // LOOK_RG
    look_rows = rows // LOOK_AZ
    share = look_rows // n
    spot_rows = -(-(kept * chips_az * tiles) // GROUP) * GROUP
    group_rows = -(-chips_az // GROUP) * GROUP
    kinds = 1 + 3 * kept
    f32 = jnp.float32
    bf16 = jnp.bfloat16
    dma = pltpu.SemaphoreType.DMA
    vmem = pl.BlockSpec(memory_space=pltpu.VMEM)
    frames = jnp.swapaxes(acquisitions, 3, 4)
    order = (0, 1, 3, 2, 4)
    coh, corr = pl.pallas_call(
        functools.partial(kernel, n, strips, (tiles, kept, chips_az, chips_rg, rows, cols)),
        out_shape=(
            jax.ShapeDtypeStruct((2, tiles, share, looks_rg, n * kept - 1), f32),
            jax.ShapeDtypeStruct((2, kept, chips_az, tiles, chips_rg), f32),
        ),
        in_specs=[pl.BlockSpec(memory_space=pltpu.HBM)] * 4,
        out_specs=(vmem, vmem),
        scratch_shapes=[
            pltpu.VMEM((kept, tiles, 2, cols + 2 * HALO, all_rows), bf16),
            pltpu.VMEM((2, kept, chips_az, tiles, chips_rg), jnp.int32),
            pltpu.VMEM((2, kept, chips_az, tiles, chips_rg), jnp.int32),
            pltpu.VMEM((1, tiles), jnp.int32),
            pltpu.VMEM((4, spot_rows, LANES), jnp.int32),
            pltpu.VMEM((chips_rg, spot_rows, LANES), f32),
            pltpu.VMEM((chips_rg, spot_rows, LANES), f32),
            pltpu.VMEM((tiles, total_units, PACK, LANES), bf16),
            pltpu.VMEM((total_units, PACK, LANES), bf16),
            pltpu.VMEM((half_units, PACK, LANES), bf16),
            pltpu.VMEM((levels, piece, PACK, LANES), bf16),
            pltpu.VMEM((levels - 1, piece, PACK, LANES), bf16),
            pltpu.VMEM((levels - 1, piece, PACK, LANES), bf16),
            pltpu.VMEM((levels * strip_piece, PACK, LANES), bf16),
            pltpu.VMEM((levels - 1, strip_piece, PACK, LANES), bf16),
            pltpu.VMEM((strip_piece, PACK, LANES), bf16),
            pltpu.VMEM((strip_piece, PACK, LANES), bf16),
            pltpu.VMEM((tiles, total_units, PACK, LANES), bf16),
            pltpu.VMEM((tiles, kept + 1, chips_az, cols, LANES), f32),
            pltpu.VMEM((2, units, PACK, LANES), bf16),
            pltpu.VMEM((2, units, PACK, LANES), bf16),
            pltpu.VMEM((2, kept * tiles * looks_rg, chips_az * LANES), f32),
            pltpu.VMEM(((kept + 1) * tiles * looks_rg, chips_az * LANES), f32),
            pltpu.VMEM((2, chips_az * LANES, LANES), bf16),
            pltpu.VMEM((n, share, LANES), f32),
            pltpu.VMEM((n, share, LANES), f32),
            pltpu.VMEM((share, n * kept + GROUP, LANES), f32),
            pltpu.VMEM((kinds, chips_rg, tiles * group_rows * GROUP, LANES), f32),
            pltpu.VMEM((chips_rg * LANES, LANES), bf16),
            dma((2,)), dma((3,)), dma((2,)), dma((2, 4)), dma((2,)), dma((6,)),
            dma((3,)), dma((3,)), dma((4,)), dma((4,)), dma((levels,)), dma((levels - 1,)),
            dma((2,)), dma((2,)), dma((1,)), dma((1,)),
        ],
        compiler_params=pltpu.CompilerParams(
            collective_id=0, has_side_effects=True, vmem_limit_bytes=50 * 1024 * 1024
        ),
    )(*[pltpu.with_memory_space_constraint(v, pltpu.HBM) for v in (frames, shifts.transpose(order), fractions.transpose(order), ref_dates[None])])
    return (corr.transpose(order), coh.transpose(0, 4, 1, 2, 3))


def solution(mesh):
    return jax.shard_map(
        functools.partial(per_device, mesh.shape["date"], mesh.shape["strip"]),
        mesh=mesh,
        in_specs=(
            P("date", None, None, None, "strip"),
            P(None, "date", None, None, "strip"),
            P(None, "date", None, None, "strip"),
            P(),
        ),
        out_specs=(P(None, "date", None, None, "strip"), P(None, None, None, "date", "strip")),
        check_vma=False,
    )
```

```python
import functools

import jax
import jax.numpy as jnp
from jax import lax
from jax.experimental import pallas as pl
from jax.experimental.pallas import tpu as pltpu
from jax.sharding import PartitionSpec as P

CHIP_SIZE = 64
TAP_COUNT = 8
SUBSTEPS = 64
LOOK_AZ = 5
LOOK_RG = 20
MARGIN = 12
LANES = 128
GROUP = 8
PACK = 16
HALO = 16
WINDOW = 96
BAND = 160
CORES = 2
SIDES = 2
EARLY = 2
SHARE = 28

epsilon = 1e-06
COS_TERMS = (1.0, -1 / 2, 1 / 24, -1 / 720, 1 / 40320, -1 / 3628800, 1 / 479001600, -1 / 87178291200)
MESH = pl.DeviceIdType.MESH


def half_turn_cos(square):
    total = jnp.full(square.shape, COS_TERMS[-1], jnp.float32)
    for term in COS_TERMS[-2::-1]:
        total = total * square + term
    return total


def tap_weights(k, fraction):
    part = fraction.astype(jnp.float32) / SUBSTEPS
    distance = k.astype(jnp.float32) - (TAP_COUNT // 2 - 1) - part
    turn = (part - 0.5) * jnp.pi
    sine = half_turn_cos(turn * turn)
    sine = jnp.where((k & 1) == 0, sine, -sine)
    sine = jnp.where(part == 0.0, 0.0, sine)
    angle = jnp.pi * distance
    sinc = jnp.where(distance == 0.0, 1.0, sine / jnp.where(distance == 0.0, 1.0, angle))
    eighth = distance * (jnp.pi / TAP_COUNT)
    window = half_turn_cos(eighth * eighth)
    weights = sinc * (window * window)
    weights = jnp.where((k >= 0) & (k < TAP_COUNT), weights, 0.0)
    return weights / jnp.sum(weights, axis=1, keepdims=True)


def spread(row, count, start):
    tall = jnp.broadcast_to(row, (count, LANES))
    return pltpu.roll(tall, start, 1, stride=1, stride_axis=0)


def split_dot(values, selector):
    high = values.astype(jnp.bfloat16)
    low = (values - high.astype(jnp.float32)).astype(jnp.bfloat16)
    return jnp.dot(high, selector, preferred_element_type=jnp.float32) + jnp.dot(
        low, selector, preferred_element_type=jnp.float32
    )


def kernel(
    n, strips, dims,
    frame_hbm, shifts_hbm, fractions_hbm, dates_hbm,
    coh_ref, corr_ref,
    frame, shifts_ref, fractions_ref, dates_ref, spots, line_base, col_base,
    cand, core_in, y_out, y_in, z_out, z_in, across_out, across_in, over, over_in, whole,
    series, sent, got, cross_sums, powers, selectors, out_buf, coh_in, ordered, totals, gather,
    load_sem, small_sem, edge_send, edge_recv, core_send, core_recv, y_send, y_recv,
    z_send, z_recv, side_recv, back_recv, next_send, next_recv, coh_send, coh_recv,
):
    tiles, kept, chips_az, chips_rg, rows, cols = dims
    me = lax.axis_index("date")
    strip = lax.axis_index("strip")
    core = me % CORES
    side = (me // CORES) % SIDES
    levels = n // (CORES * SIDES)
    level = me // (CORES * SIDES)
    bf16 = jnp.bfloat16
    f32 = jnp.float32
    chips = chips_az * chips_rg
    chip_units = CHIP_SIZE // PACK
    piece, strip_piece = y_in.shape[1], across_in.shape[1]
    half_units = levels * piece
    half_chips = half_units // chip_units
    tail_first = SIDES * half_chips
    tail = pl.ds(SIDES * half_units, levels * strip_piece)
    steps = [levels // 2] + [o for o in range(1, levels) if o != levels // 2]

    def at_level(o):
        return lax.rem(level + o, levels)

    def device(z, y, c):
        return {"date": (z * SIDES + y) * CORES + c}

    def remote(src, dst, send, recv, where):
        return pltpu.make_async_remote_copy(
            src_ref=src, dst_ref=dst, send_sem=send, recv_sem=recv,
            device_id=where, device_id_type=MESH,
        )

    inner = pl.ds(HALO, cols)
    group_rows = totals.shape[2] // (tiles * GROUP)
    dates_copy = pltpu.make_async_copy(dates_hbm, dates_ref, small_sem.at[0])
    dates_copy.start()
    loads = []
    cut = (chips_rg // 2) * CHIP_SIZE
    parts = ((1 - core, 0, cut), (1 - core, cut, cols - cut), (core, 0, cols))
    for i, (t, first, count) in enumerate(parts):
        source, target = pl.ds(first, count), pl.ds(HALO + first, count)
        loads.append(
            pltpu.make_async_copy(
                frame_hbm.at[:, t, :, source, :], frame.at[:, t, :, target, :], load_sem.at[i]
            )
        )
    loads[0].start()
    loads[1].start()
    smalls = [
        pltpu.make_async_copy(shifts_hbm, shifts_ref, small_sem.at[1]),
        pltpu.make_async_copy(fractions_hbm, fractions_ref, small_sem.at[2]),
    ]

    barrier = pltpu.get_barrier_semaphore()
    peer = me + 2 * core - 1
    has_peer = (peer >= 0) & (peer < n)
    near = [device(level, side, 1 - core), device(level, 1 - side, core)]
    near += [device(at_level(o), side, core) for o in range(1, levels)]
    for where in near:
        pl.semaphore_signal(barrier, inc=1, device_id=where, device_id_type=MESH)

    @pl.when(has_peer)
    def _():
        pl.semaphore_signal(barrier, inc=1, device_id={"date": peer}, device_id_type=MESH)

    has_low = strip > 0
    has_high = strip < strips - 1

    @pl.when(has_low)
    def _():
        pl.semaphore_signal(barrier, inc=1, device_id={"strip": strip - 1}, device_id_type=MESH)

    @pl.when(has_high)
    def _():
        pl.semaphore_signal(barrier, inc=1, device_id={"strip": strip + 1}, device_id_type=MESH)

    edge_zero = jnp.zeros((kept, tiles, 2, HALO, frame.shape[4]), bf16)

    @pl.when(strip == 0)
    def _():
        frame[:, :, :, 0:HALO, :] = edge_zero

    @pl.when(strip == strips - 1)
    def _():
        frame[:, :, :, HALO + cols : 2 * HALO + cols, :] = edge_zero

    lane = lax.broadcasted_iota(jnp.int32, (GROUP, LANES), 1)

    def wide(count):
        return lax.broadcasted_iota(jnp.int32, (count, LANES), 1)

    def half(y):
        return pl.ds(y * half_units, half_units)

    used = chips * chip_units
    spare = cand.shape[1] - used
    if spare:
        for t in range(tiles):
            cand[t, used:] = jnp.zeros((spare, PACK, LANES), bf16)

    def move(depth, start, c):
        source = lax.broadcasted_iota(jnp.int32, (depth, LANES), 0)
        target = lax.broadcasted_iota(jnp.int32, (depth, LANES), 1)
        mine = (target < CHIP_SIZE) if c == 0 else (target >= CHIP_SIZE)
        hit = mine & (source == target - c * CHIP_SIZE + start)
        return jnp.where(hit, 1.0, 0.0).astype(bf16)

    even = [move(LANES, MARGIN, c) for c in range(2)]
    odd = [move(BAND, MARGIN + CHIP_SIZE, c) for c in range(2)]

    def pick(t, first, last):
        count = (last - first) * CHIP_SIZE
        here = pl.ds(HALO + first * CHIP_SIZE, count)
        dates_row = dates_ref[0:1, :]
        date_lane = lax.broadcasted_iota(jnp.int32, (1, tiles), 1)
        date = jnp.sum(jnp.where(date_lane == t, dates_row, 0), axis=1, keepdims=True)
        gains = [
            jnp.broadcast_to(jnp.where(date == me * kept + d, 1.0, 0.0), (count, frame.shape[4]))
            .astype(bf16)
            for d in range(kept)
        ]
        parts = []
        for c in range(2):
            total = frame[0, t, c, here, :] * gains[0]
            for d in range(1, kept):
                total = total + frame[d, t, c, here, :] * gains[d]
            parts.append(total)
        for a in range(chips_az):
            start = (a // 2) * LANES
            depth = min(BAND if a % 2 else LANES, frame.shape[4] - start)
            mixed = sum(
                jnp.dot(
                    parts[c][:, start : start + depth],
                    (odd if a % 2 else even)[c][:depth],
                    preferred_element_type=f32,
                )
                for c in range(2)
            ).astype(bf16)
            for r in range(first, last):
                unit = (r * chips_az + a) * chip_units
                cand[t, unit : unit + chip_units] = mixed[
                    (r - first) * CHIP_SIZE : (r - first + 1) * CHIP_SIZE
                ].reshape(chip_units, PACK, LANES)

    dates_copy.wait()
    loads[0].wait()
    loads[2].start()
    for copy in smalls:
        copy.start()
    pick(1 - core, 0, chips_rg // 2)
    loads[1].wait()
    pick(1 - core, chips_rg // 2, chips_rg)

    beside = jnp.minimum(strip, 1) + jnp.minimum(strips - 1 - strip, 1)
    linked = jnp.where(has_peer, 1, 0)
    pl.semaphore_wait(barrier, len(near) + linked + beside)

    core_rs = [
        remote(cand.at[1 - core, span], core_in.at[span], core_send.at[0], core_recv.at[i],
               device(level, side, 1 - core))
        for i, span in enumerate((half(1 - side), tail, half(side)))
    ]
    for copy in core_rs:
        copy.start()

    order = ((core, core), (1 - core, 1 - core), (core, 1 - core), (1 - core, core))
    edges = []
    for i, (d, t) in enumerate(order):
        up = remote(
            frame_hbm.at[d, t, :, pl.ds(cols - HALO, HALO), :], frame.at[d, t, :, pl.ds(0, HALO), :],
            edge_send.at[0], edge_recv.at[0, i], {"strip": strip + 1},
        )
        down = remote(
            frame_hbm.at[d, t, :, pl.ds(0, HALO), :], frame.at[d, t, :, pl.ds(HALO + cols, HALO), :],
            edge_send.at[1], edge_recv.at[1, i], {"strip": strip - 1},
        )
        edges.append((up, down))

        @pl.when(has_high)
        def _():
            up.start()

        @pl.when(has_low)
        def _():
            down.start()

    def edge_wait(i):
        @pl.when(has_low)
        def _():
            edges[i][0].wait_recv()

        @pl.when(has_high)
        def _():
            edges[i][1].wait_recv()

    loads[2].wait()
    pick(core, 0, chips_rg)

    def level_piece(y, z):
        return pl.ds(y * half_units + z * piece, piece)

    y_rs = [
        remote(y_out.at[level_piece(0, at_level(o))], y_in.at[k], y_send.at[0], side_recv.at[k],
               device(level, 1 - side, core))
        for k, o in enumerate(steps + [0])
    ]
    z_rs = [
        remote(z_out.at[k], z_in.at[k], z_send.at[0], z_recv.at[0],
               device(at_level(o), side, core))
        for k, o in enumerate(steps)
    ]
    mine = whole.at[core, level_piece(side, level)]
    z_ag = [
        remote(mine, mine, z_send.at[1], back_recv.at[k], device(at_level(o), side, core))
        for k, o in enumerate(steps)
    ]
    y_ag = []
    for k, o in enumerate(steps + [0]):
        part = whole.at[core, level_piece(side, at_level(levels - o))]
        y_ag.append(
            remote(part, part, y_send.at[1], y_recv.at[1], device(level, 1 - side, core))
        )
    core_ag = [
        remote(whole.at[core, span], whole.at[core, span], core_send.at[1], core_recv.at[3 + i],
               device(level, side, 1 - core))
        for i, span in enumerate((half(side), half(1 - side), tail))
    ]

    def tail_piece(z):
        return pl.ds(SIDES * half_units + z * strip_piece, strip_piece)

    tail_rs = [
        remote(across_out.at[pl.ds(at_level(o) * strip_piece, strip_piece)], across_in.at[k],
               z_send.at[2], z_recv.at[2], device(at_level(o), side, core))
        for k, o in enumerate(steps)
    ]
    tail_y = remote(over, over_in, y_send.at[2], y_recv.at[2], device(level, 1 - side, core))
    tail_mine = whole.at[core, tail_piece(level)]
    tail_ag = [
        remote(tail_mine, tail_mine, z_send.at[3], z_recv.at[3], device(at_level(o), side, core))
        for o in steps
    ]

    def all_of(ref, send, recv):
        return remote(ref, ref, send, recv, device(level, side, core))

    def tail_core():
        core_rs[1].wait_recv()
        across_out[...] = cand[core, tail] + core_in[tail]
        for copy in tail_rs:
            copy.start()

    def tail_side():
        all_of(across_in, z_send.at[2], z_recv.at[2]).wait_recv()
        total = across_out[pl.ds(level * strip_piece, strip_piece)]
        for k in range(len(steps)):
            total = total + across_in[k]
        over[...] = total
        tail_y.start()

    def tail_level():
        tail_y.wait_recv()
        whole[core, tail_piece(level)] = over[...] + over_in[...]
        for copy in tail_ag:
            copy.start()

    def tail_back():
        all_of(across_in, z_send.at[3], z_recv.at[3]).wait_recv()
        core_ag[2].start()

    def ref_core():
        core_rs[0].wait_recv()
        y_out[...] = cand[core, half(1 - side)] + core_in[half(1 - side)]
        for copy in y_rs:
            copy.start()

    def piece_sum(k, o):
        at = level_piece(side, at_level(o))
        y_rs[k].wait_recv()
        return cand[core, at] + core_in[at] + y_in[k]

    def ref_side(k):
        if k == 0:
            core_rs[2].wait_recv()
        z_out[k] = piece_sum(k, steps[k])
        z_rs[k].start()

    def ref_level():
        total = piece_sum(len(steps), 0)
        all_of(z_in, z_send.at[0], z_recv.at[0]).wait_recv()
        for k in range(len(steps)):
            total = total + z_in[k]
        whole[core, level_piece(side, level)] = total
        for copy in z_ag:
            copy.start()
        y_ag[len(steps)].start()

    def ref_back(k):
        z_ag[k].wait_recv()
        y_ag[k].start()
        if k == len(steps) - 1:
            core_ag[0].start()

    def ref_other():
        all_of(y_out, y_send.at[1], y_recv.at[1]).wait_recv()
        core_ag[1].start()

    ref_core()
    tail_core()

    smalls[0].wait()
    smalls[1].wait()

    for d in range(kept):
        for a in range(chips_az):
            row = (d * chips_az + a) * tiles
            for i in range(2):
                spots[i, row : row + tiles, :chips_rg] = shifts_ref[i, d, a]
                spots[2 + i, row : row + tiles, :chips_rg] = fractions_ref[i, d, a]
    spot_rows = kept * chips_az * tiles
    first_tap = MARGIN - TAP_COUNT // 2 + 1
    at = wide(spot_rows)
    for r in range(chips_rg):
        values = [
            jnp.broadcast_to(spots[i, 0:spot_rows, r : r + 1], (spot_rows, LANES)) for i in range(4)
        ]
        line_tap = ((LANES - at) & (LANES - 1)) - (values[0] + first_tap)
        line_base[r, 0:spot_rows, :] = tap_weights(line_tap, values[2])
        col_tap = at - (values[1] + (first_tap + HALO - MARGIN))
        col_base[r, 0:spot_rows, :] = tap_weights(col_tap, values[3])

    low_lane = wide(CHIP_SIZE) < CHIP_SIZE

    def halves(count):
        return wide(count) < CHIP_SIZE

    def chip_column(d, t, r, slot):
        row0 = r * CHIP_SIZE
        window = pl.ds(row0, WINDOW)

        def base(ref, a):
            return ref[r, pl.ds((d * chips_az + a) * tiles + t, 1), :]

        partial = [None] * chips_az
        reach = CHIP_SIZE + 2 * MARGIN
        for a in range(0, chips_az - 1, 2):
            b = a // 2
            span = slice(b * LANES, b * LANES + BAND)
            image = jnp.concatenate([frame[d, t, c, window, span] for c in range(2)], axis=0)
            first = spread(base(line_base, a), reach, 0)
            second = spread(base(line_base, a + 1), BAND - CHIP_SIZE, CHIP_SIZE)
            shared = reach - CHIP_SIZE
            matrix = jnp.concatenate(
                [
                    jnp.where(halves(CHIP_SIZE), first[:CHIP_SIZE], 0.0),
                    jnp.where(halves(shared), first[CHIP_SIZE:], second[:shared]),
                    jnp.where(halves(BAND - reach), 0.0, second[shared:]),
                ],
                axis=0,
            ).astype(bf16)
            out = jnp.dot(image, matrix, preferred_element_type=f32)
            re, im = out[:WINDOW], out[WINDOW:]
            left = halves(WINDOW)
            partial[a] = jnp.where(left, re, pltpu.roll(im, CHIP_SIZE, 1)).astype(bf16)
            partial[a + 1] = jnp.where(left, pltpu.roll(re, CHIP_SIZE, 1), im).astype(bf16)
        if chips_az % 2:
            a = chips_az - 1
            span = slice(a * CHIP_SIZE, a * CHIP_SIZE + reach)
            row = base(line_base, a)
            left = halves(reach)
            top = jnp.where(left, spread(row, reach, 0), 0.0).astype(bf16)
            bottom = jnp.where(left, 0.0, spread(row, reach, CHIP_SIZE)).astype(bf16)
            partial[a] = (
                jnp.dot(frame[d, t, 0, window, span], top, preferred_element_type=f32)
                + jnp.dot(frame[d, t, 1, window, span], bottom, preferred_element_type=f32)
            ).astype(bf16)
        for a in range(chips_az):
            matrix = spread(base(col_base, a), CHIP_SIZE, 0)[:, :WINDOW].astype(bf16)
            out = jnp.dot(matrix, partial[a], preferred_element_type=f32).astype(bf16)
            if slot is not None:
                unit = (r * chips_az + a) * chip_units
                sent[slot, pl.ds(unit, chip_units)] = out.reshape(chip_units, PACK, LANES)
            out = out.astype(f32)
            series[t, d + t, a, pl.ds(row0, CHIP_SIZE), :] = out
            power = jnp.sum((out * out).reshape(GROUP, GROUP, LANES), axis=0)
            totals[1 + 2 * kept + d, r, pl.ds((t * group_rows + a) * GROUP, GROUP), :] = power

    def resample(i, first, last):
        d, t = order[i]

        for j in range(first, last):
            chip_column(d, t, (j + 1) % chips_rg, i if i < 2 else None)

    inside_cols = chips_rg - 2
    column = chips_az * chip_units
    outward = []
    for r in range(chips_rg):
        span = pl.ds(r * column, column)
        outward.append(
            remote(sent.at[0, span], got.at[0, span], next_send.at[0], next_recv.at[0], {"date": peer})
        )

    def outward_start(first, last):
        @pl.when(has_peer)
        def _():
            for r in range(first, last):
                outward[(r + 1) % chips_rg].start()

    def outward_all():
        return remote(sent.at[0], got.at[0], next_send.at[0], next_recv.at[0], {"date": peer})

    inward = remote(
        sent.at[1], got.at[1], next_send.at[1], next_recv.at[1], device(level, side, 1 - core)
    )

    resample(0, 0, inside_cols)
    ref_side(0)
    edge_wait(0)
    resample(0, inside_cols, chips_rg)
    ref_side(1)
    outward_start(0, EARLY)
    resample(1, 0, inside_cols)
    for k in range(2, len(steps)):
        ref_side(k)
    outward_start(EARLY, 3)
    edge_wait(1)
    resample(1, inside_cols, chips_rg)
    inward.start()
    tail_side()
    outward_start(3, chips_rg)
    resample(2, 0, inside_cols)
    edge_wait(2)
    resample(2, inside_cols, chips_rg)
    ref_level()
    resample(3, 0, inside_cols)
    edge_wait(3)
    resample(3, inside_cols, chips_rg)

    looks_rg = cols // LOOK_RG
    look_rows = rows // LOOK_AZ

    def pick_rows(t, pos, a, s):
        return series[t, pos, a, pl.ds(s, looks_rg, stride=LOOK_RG), :]

    def look(t, early, wanted):
        for a in range(chips_az):
            sums = [jnp.zeros((looks_rg, LANES), f32) for _ in range(2 + len(wanted))]
            for s in range(LOOK_RG):
                first = pick_rows(t, early, a, s)
                second = pick_rows(t, early + 1, a, s)
                sums[0] = sums[0] + first * second
                sums[1] = sums[1] + first * pltpu.roll(second, CHIP_SIZE, 1)
                for i, pos in enumerate(wanted):
                    value = pick_rows(t, pos, a, s)
                    sums[2 + i] = sums[2 + i] + value * value
            span = slice(a * LANES, (a + 1) * LANES)
            row = pl.multiple_of((early * tiles + t) * looks_rg, GROUP)
            for c in range(2):
                cross_sums[c, pl.ds(row, looks_rg), span] = sums[c]
            for i, pos in enumerate(wanted):
                row = pl.multiple_of((pos * tiles + t) * looks_rg, GROUP)
                powers[pl.ds(row, looks_rg), span] = sums[2 + i]

    def unpack(i, t, pos):
        def body(j, carry):
            for a in range(chips_az):
                unit = (j * chips_az + a) * chip_units
                value = got[i, pl.ds(unit, chip_units)].reshape(CHIP_SIZE, LANES)
                row = pl.multiple_of(j * CHIP_SIZE, CHIP_SIZE)
                series[t, pos, a, pl.ds(row, CHIP_SIZE), :] = value.astype(f32)
            return carry

        lax.fori_loop(0, chips_rg, body, 0)

    look(1 - core, 1 - core, (1 - core, 2 - core))

    def build_selectors(a, carry):
        line = lax.broadcasted_iota(jnp.int32, (LANES, LANES), 0)
        y = lax.broadcasted_iota(jnp.int32, (LANES, LANES), 1)
        gap = a * CHIP_SIZE + (line & (CHIP_SIZE - 1)) - LOOK_AZ * y
        hit = (gap >= 0) & (gap < LOOK_AZ)
        span = pl.ds(pl.multiple_of(a * LANES, LANES), LANES)
        selectors[0, span, :] = jnp.where(hit, 1.0, 0.0).astype(bf16)
        selectors[1, span, :] = jnp.where(
            hit, jnp.where(line < CHIP_SIZE, -1.0, 1.0), 0.0
        ).astype(bf16)
        return carry

    lax.fori_loop(0, chips_az, build_selectors, 0)
    source = lax.broadcasted_iota(jnp.int32, gather.shape, 0)
    target = lax.broadcasted_iota(jnp.int32, gather.shape, 1)
    gap = source - target * LANES
    gather[...] = jnp.where((gap >= 0) & (gap < LANES), 1.0, 0.0).astype(bf16)

    def correlate(t, first, count):
        for j in range(count):
            chip = first + j
            a = chip % chips_az
            r = chip // chips_az
            row = pl.multiple_of(r * CHIP_SIZE, CHIP_SIZE)
            to = pl.ds(pl.multiple_of((t * group_rows + a) * GROUP, GROUP), GROUP)
            sums = [None] * (1 + 2 * kept)
            for g in range(chip_units):
                ref = whole[t, chip * chip_units + g].astype(f32)
                turned = pltpu.roll(ref, CHIP_SIZE, 1)
                terms = [ref * ref]
                for d in range(kept):
                    value = series[t, d + t, a, pl.ds(row + g * PACK, PACK), :]
                    terms += [ref * value, turned * value]
                for k, term in enumerate(terms):
                    term = term[:GROUP] + term[GROUP:]
                    sums[k] = term if sums[k] is None else sums[k] + term
            for k, value in enumerate(sums):
                totals[k, r, to, :] = value

    look(core, core, (core, 1 + core))
    inward.wait_recv()
    unpack(1, core, 2 * (1 - core))
    look(core, 1 - core, (2 * (1 - core),))

    for k in range(2):
        ref_back(k)
    tail_level()

    @pl.when(has_peer)
    def _():
        outward_all().wait_recv()
        unpack(0, 1 - core, 2 * core)

    @pl.when(jnp.logical_not(has_peer))
    def _():
        series[1 - core, 2 * core] = jnp.zeros(series.shape[2:], f32)

    look(1 - core, core, (2 * core,))

    summed = [split_dot(cross_sums[c], selectors[c]) for c in range(2)]
    power = split_dot(powers[...], selectors[0])
    count = kept * tiles * looks_rg
    skip = tiles * looks_rg
    scale = jnp.sqrt((power[:count] + epsilon) * (power[skip : skip + count] + epsilon))
    coherence = jnp.concatenate([v / scale for v in summed], axis=0).T
    share = look_rows // n
    for j in range(n):
        out_buf[j] = coherence[j * share : (j + 1) * share]
    coh_in[me] = out_buf[me]
    for o in range(1, n):
        to = lax.rem(me + o, n)
        copy = remote(
            out_buf.at[to], coh_in.at[me], coh_send.at[0], coh_recv.at[0], {"date": to}
        )
        copy.start()

    for k in range(2, len(steps)):
        ref_back(k)
    tail_back()
    tail_chips = chips - tail_first
    correlate(core, side * half_chips, half_chips)
    correlate(core, tail_first, tail_chips)
    core_ag[0].wait_recv()
    correlate(1 - core, side * half_chips, half_chips)
    core_ag[2].wait_recv()
    correlate(1 - core, tail_first, tail_chips)
    ref_other()
    kinds = totals.shape[0]

    def finish(t):
        sign = jnp.where(wide(group_rows) < CHIP_SIZE, 1.0, -1.0).astype(f32)
        folded = []
        for k in range(kinds):
            line = []
            for r in range(chips_rg):
                total = None
                for s in range(GROUP):
                    at = pl.ds(t * (group_rows * GROUP) + s, group_rows, stride=GROUP)
                    value = totals[k, r, at, :]
                    total = value if total is None else total + value
                if 1 <= k <= 2 * kept and k % 2 == 0:
                    total = total * sign
                line.append(total)
            folded.append(jnp.concatenate(line, axis=1))
        sums = split_dot(jnp.concatenate(folded, axis=0), gather[...])
        sums = [sums[k * group_rows : (k + 1) * group_rows] for k in range(kinds)]
        for d in range(kept):
            scale = jnp.sqrt((sums[0] + epsilon) * (sums[1 + 2 * kept + d] + epsilon))
            for c in range(2):
                value = sums[1 + 2 * d + c] / scale
                for a in range(chips_az):
                    corr_ref[c, d, a, pl.ds(t, 1), :] = value[a : a + 1, :chips_rg]

    correlate(core, (1 - side) * half_chips, half_chips)
    finish(core)

    others = pl.ds(0, n - 1)
    relays = remote(
        out_buf.at[others], coh_in.at[others], coh_send.at[0], coh_recv.at[0], {"date": me}
    )
    relays.wait_recv()
    pairs = n * kept
    lane_n = wide(n)
    for y in range(share):
        value = coh_in[:, y, :]
        ordered[y, pl.ds(0, n, stride=2), :] = value
        ordered[y, pl.ds(1, n, stride=2), :] = pltpu.roll(value, LANES - tiles * looks_rg, 1)
    lane_p = wide(pairs)
    for y in range(share):
        first = (lane_p & (2 * looks_rg - 1)) < looks_rg
        value = jnp.where(first, ordered[y, 0:pairs, :], ordered[y, 1 : pairs + 1, :]).T
        for c in range(2):
            for t in range(tiles):
                row = c * kept * tiles * looks_rg + t * looks_rg
                coh_ref[c, t, y] = value[row : row + looks_rg, : pairs - 1]

    core_ag[1].wait_recv()
    correlate(1 - core, (1 - side) * half_chips, half_chips)
    finish(1 - core)

    relays.wait_send()
    inward.wait_send()
    for ref, sem in (
        (cand.at[1 - core], core_send.at[0]),
        (whole.at[core], core_send.at[1]),
        (y_out, y_send.at[0]),
        (y_out, y_send.at[1]),
        (over, y_send.at[2]),
        (z_out, z_send.at[0]),
        (z_out, z_send.at[1]),
        (across_in, z_send.at[2]),
        (across_in, z_send.at[3]),
    ):
        all_of(ref, sem, sem).wait_send()

    @pl.when(has_peer)
    def _():
        outward_all().wait_send()

    rim = frame.at[:, :, :, 0:HALO, :]

    @pl.when(has_high)
    def _():
        all_of(rim, edge_send.at[0], edge_send.at[0]).wait_send()

    @pl.when(has_low)
    def _():
        all_of(rim, edge_send.at[1], edge_send.at[1]).wait_send()


def per_device(n, strips, acquisitions, shifts, fractions, ref_dates):
    kept, tiles, _, all_rows, cols = acquisitions.shape
    rows = all_rows - 2 * MARGIN
    chips_az, chips_rg = shifts.shape[3:]
    chips = chips_az * chips_rg
    units = chips * CHIP_SIZE // PACK
    levels = n // (CORES * SIDES)
    piece = max(units * SHARE // 100 // levels, 1)
    half_units = piece * levels
    strip_piece = -(-(units - SIDES * half_units) // levels)
    total_units = SIDES * half_units + levels * strip_piece
    looks_rg = cols // LOOK_RG
    look_rows = rows // LOOK_AZ
    share = look_rows // n
    spot_rows = -(-(kept * chips_az * tiles) // GROUP) * GROUP
    group_rows = -(-chips_az // GROUP) * GROUP
    kinds = 1 + 3 * kept
    f32 = jnp.float32
    bf16 = jnp.bfloat16
    dma = pltpu.SemaphoreType.DMA
    vmem = pl.BlockSpec(memory_space=pltpu.VMEM)
    frames = jnp.swapaxes(acquisitions, 3, 4)
    order = (0, 1, 3, 2, 4)
    coh, corr = pl.pallas_call(
        functools.partial(kernel, n, strips, (tiles, kept, chips_az, chips_rg, rows, cols)),
        out_shape=(
            jax.ShapeDtypeStruct((2, tiles, share, looks_rg, n * kept - 1), f32),
            jax.ShapeDtypeStruct((2, kept, chips_az, tiles, chips_rg), f32),
        ),
        in_specs=[pl.BlockSpec(memory_space=pltpu.HBM)] * 4,
        out_specs=(vmem, vmem),
        scratch_shapes=[
            pltpu.VMEM((kept, tiles, 2, cols + 2 * HALO, all_rows), bf16),
            pltpu.VMEM((2, kept, chips_az, tiles, chips_rg), jnp.int32),
            pltpu.VMEM((2, kept, chips_az, tiles, chips_rg), jnp.int32),
            pltpu.VMEM((1, tiles), jnp.int32),
            pltpu.VMEM((4, spot_rows, LANES), jnp.int32),
            pltpu.VMEM((chips_rg, spot_rows, LANES), f32),
            pltpu.VMEM((chips_rg, spot_rows, LANES), f32),
            pltpu.VMEM((tiles, total_units, PACK, LANES), bf16),
            pltpu.VMEM((total_units, PACK, LANES), bf16),
            pltpu.VMEM((half_units, PACK, LANES), bf16),
            pltpu.VMEM((levels, piece, PACK, LANES), bf16),
            pltpu.VMEM((levels - 1, piece, PACK, LANES), bf16),
            pltpu.VMEM((levels - 1, piece, PACK, LANES), bf16),
            pltpu.VMEM((levels * strip_piece, PACK, LANES), bf16),
            pltpu.VMEM((levels - 1, strip_piece, PACK, LANES), bf16),
            pltpu.VMEM((strip_piece, PACK, LANES), bf16),
            pltpu.VMEM((strip_piece, PACK, LANES), bf16),
            pltpu.VMEM((tiles, total_units, PACK, LANES), bf16),
            pltpu.VMEM((tiles, kept + 1, chips_az, cols, LANES), f32),
            pltpu.VMEM((2, units, PACK, LANES), bf16),
            pltpu.VMEM((2, units, PACK, LANES), bf16),
            pltpu.VMEM((2, kept * tiles * looks_rg, chips_az * LANES), f32),
            pltpu.VMEM(((kept + 1) * tiles * looks_rg, chips_az * LANES), f32),
            pltpu.VMEM((2, chips_az * LANES, LANES), bf16),
            pltpu.VMEM((n, share, LANES), f32),
            pltpu.VMEM((n, share, LANES), f32),
            pltpu.VMEM((share, n * kept + GROUP, LANES), f32),
            pltpu.VMEM((kinds, chips_rg, tiles * group_rows * GROUP, LANES), f32),
            pltpu.VMEM((chips_rg * LANES, LANES), bf16),
            dma((3,)), dma((3,)), dma((2,)), dma((2, 4)), dma((2,)), dma((6,)),
            dma((3,)), dma((3,)), dma((4,)), dma((4,)), dma((levels,)), dma((levels - 1,)),
            dma((2,)), dma((2,)), dma((1,)), dma((1,)),
        ],
        compiler_params=pltpu.CompilerParams(
            collective_id=0, has_side_effects=True, vmem_limit_bytes=50 * 1024 * 1024
        ),
    )(*[pltpu.with_memory_space_constraint(v, pltpu.HBM) for v in (frames, shifts.transpose(order), fractions.transpose(order), ref_dates[None])])
    return (corr.transpose(order), coh.transpose(0, 4, 1, 2, 3))


def solution(mesh):
    return jax.shard_map(
        functools.partial(per_device, mesh.shape["date"], mesh.shape["strip"]),
        mesh=mesh,
        in_specs=(
            P("date", None, None, None, "strip"),
            P(None, "date", None, None, "strip"),
            P(None, "date", None, None, "strip"),
            P(),
        ),
        out_specs=(P(None, "date", None, None, "strip"), P(None, None, None, "date", "strip")),
        check_vma=False,
    )
```

```python
import functools

import jax
import jax.numpy as jnp
from jax import lax
from jax.experimental import pallas as pl
from jax.experimental.pallas import tpu as pltpu
from jax.sharding import PartitionSpec as P

CHIP_SIZE = 64
TAP_COUNT = 8
SUBSTEPS = 64
LOOK_AZ = 5
LOOK_RG = 20
MARGIN = 12
LANES = 128
GROUP = 8
PACK = 16
HALO = 16
WINDOW = 96
BAND = 160
CORES = 2
SIDES = 2
EARLY = 2
SHARE = 28

epsilon = 1e-06
COS_TERMS = (1.0, -1 / 2, 1 / 24, -1 / 720, 1 / 40320, -1 / 3628800, 1 / 479001600, -1 / 87178291200)
MESH = pl.DeviceIdType.MESH


def half_turn_cos(square):
    total = jnp.full(square.shape, COS_TERMS[-1], jnp.float32)
    for term in COS_TERMS[-2::-1]:
        total = total * square + term
    return total


def tap_weights(k, fraction):
    part = fraction.astype(jnp.float32) / SUBSTEPS
    distance = k.astype(jnp.float32) - (TAP_COUNT // 2 - 1) - part
    turn = (part - 0.5) * jnp.pi
    sine = half_turn_cos(turn * turn)
    sine = jnp.where((k & 1) == 0, sine, -sine)
    sine = jnp.where(part == 0.0, 0.0, sine)
    angle = jnp.pi * distance
    sinc = jnp.where(distance == 0.0, 1.0, sine / jnp.where(distance == 0.0, 1.0, angle))
    eighth = distance * (jnp.pi / TAP_COUNT)
    window = half_turn_cos(eighth * eighth)
    weights = sinc * (window * window)
    weights = jnp.where((k >= 0) & (k < TAP_COUNT), weights, 0.0)
    return weights / jnp.sum(weights, axis=1, keepdims=True)


def spread(row, count, start):
    tall = jnp.broadcast_to(row, (count, LANES))
    return pltpu.roll(tall, start, 1, stride=1, stride_axis=0)


def split_dot(values, selector):
    high = values.astype(jnp.bfloat16)
    low = (values - high.astype(jnp.float32)).astype(jnp.bfloat16)
    return jnp.dot(high, selector, preferred_element_type=jnp.float32) + jnp.dot(
        low, selector, preferred_element_type=jnp.float32
    )


def kernel(
    n, strips, dims,
    frame_hbm, shifts_hbm, fractions_hbm, dates_hbm,
    coh_ref, corr_ref,
    frame, shifts_ref, fractions_ref, dates_ref, spots, line_base, col_base,
    cand, core_in, y_out, y_in, z_out, z_in, across_out, across_in, over, over_in, whole,
    series, sent, got, cross_sums, powers, selectors, out_buf, coh_in, ordered, totals, gather,
    load_sem, small_sem, edge_send, edge_recv, core_send, core_recv, y_send, y_recv,
    z_send, z_recv, side_recv, back_recv, next_send, next_recv, coh_send, coh_recv,
):
    tiles, kept, chips_az, chips_rg, rows, cols = dims
    me = lax.axis_index("date")
    strip = lax.axis_index("strip")
    core = me % CORES
    side = (me // CORES) % SIDES
    levels = n // (CORES * SIDES)
    level = me // (CORES * SIDES)
    bf16 = jnp.bfloat16
    f32 = jnp.float32
    chips = chips_az * chips_rg
    chip_units = CHIP_SIZE // PACK
    piece, strip_piece = y_in.shape[1], across_in.shape[1]
    half_units = levels * piece
    half_chips = half_units // chip_units
    tail_first = SIDES * half_chips
    tail = pl.ds(SIDES * half_units, levels * strip_piece)
    steps = [levels // 2] + [o for o in range(1, levels) if o != levels // 2]

    def at_level(o):
        return lax.rem(level + o, levels)

    def device(z, y, c):
        return {"date": (z * SIDES + y) * CORES + c}

    def remote(src, dst, send, recv, where):
        return pltpu.make_async_remote_copy(
            src_ref=src, dst_ref=dst, send_sem=send, recv_sem=recv,
            device_id=where, device_id_type=MESH,
        )

    inner = pl.ds(HALO, cols)
    group_rows = totals.shape[2] // (tiles * GROUP)
    dates_copy = pltpu.make_async_copy(dates_hbm, dates_ref, small_sem.at[0])
    dates_copy.start()
    loads = []
    cut = (chips_rg // 2) * CHIP_SIZE
    parts = ((1 - core, 0, cut), (1 - core, cut, cols - cut), (core, 0, cols))
    for i, (t, first, count) in enumerate(parts):
        source, target = pl.ds(first, count), pl.ds(HALO + first, count)
        loads.append(
            pltpu.make_async_copy(
                frame_hbm.at[:, t, :, source, :], frame.at[:, t, :, target, :], load_sem.at[i]
            )
        )
    loads[0].start()
    loads[1].start()
    smalls = [
        pltpu.make_async_copy(shifts_hbm, shifts_ref, small_sem.at[1]),
        pltpu.make_async_copy(fractions_hbm, fractions_ref, small_sem.at[2]),
    ]

    barrier = pltpu.get_barrier_semaphore()
    peer = me + 2 * core - 1
    has_peer = (peer >= 0) & (peer < n)
    near = [device(level, side, 1 - core), device(level, 1 - side, core)]
    near += [device(at_level(o), side, core) for o in range(1, levels)]
    for where in near:
        pl.semaphore_signal(barrier, inc=1, device_id=where, device_id_type=MESH)

    @pl.when(has_peer)
    def _():
        pl.semaphore_signal(barrier, inc=1, device_id={"date": peer}, device_id_type=MESH)

    has_low = strip > 0
    has_high = strip < strips - 1

    @pl.when(has_low)
    def _():
        pl.semaphore_signal(barrier, inc=1, device_id={"strip": strip - 1}, device_id_type=MESH)

    @pl.when(has_high)
    def _():
        pl.semaphore_signal(barrier, inc=1, device_id={"strip": strip + 1}, device_id_type=MESH)

    edge_zero = jnp.zeros((kept, tiles, 2, HALO, frame.shape[4]), bf16)

    @pl.when(strip == 0)
    def _():
        frame[:, :, :, 0:HALO, :] = edge_zero

    @pl.when(strip == strips - 1)
    def _():
        frame[:, :, :, HALO + cols : 2 * HALO + cols, :] = edge_zero

    lane = lax.broadcasted_iota(jnp.int32, (GROUP, LANES), 1)

    def wide(count):
        return lax.broadcasted_iota(jnp.int32, (count, LANES), 1)

    def half(y):
        return pl.ds(y * half_units, half_units)

    used = chips * chip_units
    spare = cand.shape[1] - used
    if spare:
        for t in range(tiles):
            cand[t, used:] = jnp.zeros((spare, PACK, LANES), bf16)

    def move(depth, start, c):
        source = lax.broadcasted_iota(jnp.int32, (depth, LANES), 0)
        target = lax.broadcasted_iota(jnp.int32, (depth, LANES), 1)
        mine = (target < CHIP_SIZE) if c == 0 else (target >= CHIP_SIZE)
        hit = mine & (source == target - c * CHIP_SIZE + start)
        return jnp.where(hit, 1.0, 0.0).astype(bf16)

    even = [move(LANES, MARGIN, c) for c in range(2)]
    odd = [move(BAND, MARGIN + CHIP_SIZE, c) for c in range(2)]

    def pick(t, first, last):
        count = (last - first) * CHIP_SIZE
        here = pl.ds(HALO + first * CHIP_SIZE, count)
        dates_row = dates_ref[0:1, :]
        date_lane = lax.broadcasted_iota(jnp.int32, (1, tiles), 1)
        date = jnp.sum(jnp.where(date_lane == t, dates_row, 0), axis=1, keepdims=True)
        gains = [
            jnp.broadcast_to(jnp.where(date == me * kept + d, 1.0, 0.0), (count, frame.shape[4]))
            .astype(bf16)
            for d in range(kept)
        ]
        parts = []
        for c in range(2):
            total = frame[0, t, c, here, :] * gains[0]
            for d in range(1, kept):
                total = total + frame[d, t, c, here, :] * gains[d]
            parts.append(total)
        for a in range(chips_az):
            start = (a // 2) * LANES
            depth = min(BAND if a % 2 else LANES, frame.shape[4] - start)
            mixed = sum(
                jnp.dot(
                    parts[c][:, start : start + depth],
                    (odd if a % 2 else even)[c][:depth],
                    preferred_element_type=f32,
                )
                for c in range(2)
            ).astype(bf16)
            for r in range(first, last):
                unit = (r * chips_az + a) * chip_units
                cand[t, unit : unit + chip_units] = mixed[
                    (r - first) * CHIP_SIZE : (r - first + 1) * CHIP_SIZE
                ].reshape(chip_units, PACK, LANES)

    dates_copy.wait()
    loads[0].wait()
    loads[2].start()
    for copy in smalls:
        copy.start()
    pick(1 - core, 0, chips_rg // 2)
    loads[1].wait()
    pick(1 - core, chips_rg // 2, chips_rg)

    beside = jnp.minimum(strip, 1) + jnp.minimum(strips - 1 - strip, 1)
    linked = jnp.where(has_peer, 1, 0)
    pl.semaphore_wait(barrier, len(near) + linked + beside)

    core_rs = [
        remote(cand.at[1 - core, span], core_in.at[span], core_send.at[0], core_recv.at[i],
               device(level, side, 1 - core))
        for i, span in enumerate((half(1 - side), tail, half(side)))
    ]
    for copy in core_rs:
        copy.start()

    order = ((core, core), (1 - core, 1 - core), (core, 1 - core), (1 - core, core))
    edges = []
    for i, (d, t) in enumerate(order):
        up = remote(
            frame_hbm.at[d, t, :, pl.ds(cols - HALO, HALO), :], frame.at[d, t, :, pl.ds(0, HALO), :],
            edge_send.at[0], edge_recv.at[0, i], {"strip": strip + 1},
        )
        down = remote(
            frame_hbm.at[d, t, :, pl.ds(0, HALO), :], frame.at[d, t, :, pl.ds(HALO + cols, HALO), :],
            edge_send.at[1], edge_recv.at[1, i], {"strip": strip - 1},
        )
        edges.append((up, down))

        @pl.when(has_high)
        def _():
            up.start()

        @pl.when(has_low)
        def _():
            down.start()

    def edge_wait(i):
        @pl.when(has_low)
        def _():
            edges[i][0].wait_recv()

        @pl.when(has_high)
        def _():
            edges[i][1].wait_recv()

    loads[2].wait()
    pick(core, 0, chips_rg)

    def level_piece(y, z):
        return pl.ds(y * half_units + z * piece, piece)

    y_rs = [
        remote(y_out.at[level_piece(0, at_level(o))], y_in.at[k], y_send.at[0], side_recv.at[k],
               device(level, 1 - side, core))
        for k, o in enumerate(steps + [0])
    ]
    z_rs = [
        remote(z_out.at[k], z_in.at[k], z_send.at[0], z_recv.at[0],
               device(at_level(o), side, core))
        for k, o in enumerate(steps)
    ]
    mine = whole.at[core, level_piece(side, level)]
    z_ag = [
        remote(mine, mine, z_send.at[1], back_recv.at[k], device(at_level(o), side, core))
        for k, o in enumerate(steps)
    ]
    y_ag = []
    for k, o in enumerate(steps + [0]):
        part = whole.at[core, level_piece(side, at_level(levels - o))]
        y_ag.append(
            remote(part, part, y_send.at[1], y_recv.at[1], device(level, 1 - side, core))
        )
    core_ag = [
        remote(whole.at[core, span], whole.at[core, span], core_send.at[1], core_recv.at[3 + i],
               device(level, side, 1 - core))
        for i, span in enumerate((half(side), half(1 - side), tail))
    ]

    def tail_piece(z):
        return pl.ds(SIDES * half_units + z * strip_piece, strip_piece)

    tail_rs = [
        remote(across_out.at[pl.ds(at_level(o) * strip_piece, strip_piece)], across_in.at[k],
               z_send.at[2], z_recv.at[2], device(at_level(o), side, core))
        for k, o in enumerate(steps)
    ]
    tail_y = remote(over, over_in, y_send.at[2], y_recv.at[2], device(level, 1 - side, core))
    tail_mine = whole.at[core, tail_piece(level)]
    tail_ag = [
        remote(tail_mine, tail_mine, z_send.at[3], z_recv.at[3], device(at_level(o), side, core))
        for o in steps
    ]

    def all_of(ref, send, recv):
        return remote(ref, ref, send, recv, device(level, side, core))

    def tail_core():
        core_rs[1].wait_recv()
        across_out[...] = cand[core, tail] + core_in[tail]
        for copy in tail_rs:
            copy.start()

    def tail_side():
        all_of(across_in, z_send.at[2], z_recv.at[2]).wait_recv()
        total = across_out[pl.ds(level * strip_piece, strip_piece)]
        for k in range(len(steps)):
            total = total + across_in[k]
        over[...] = total
        tail_y.start()

    def tail_level():
        tail_y.wait_recv()
        whole[core, tail_piece(level)] = over[...] + over_in[...]
        for copy in tail_ag:
            copy.start()

    def tail_back():
        all_of(across_in, z_send.at[3], z_recv.at[3]).wait_recv()
        core_ag[2].start()

    def ref_core():
        core_rs[0].wait_recv()
        y_out[...] = cand[core, half(1 - side)] + core_in[half(1 - side)]
        for copy in y_rs:
            copy.start()

    def piece_sum(k, o):
        at = level_piece(side, at_level(o))
        y_rs[k].wait_recv()
        return cand[core, at] + core_in[at] + y_in[k]

    def ref_side(k):
        if k == 0:
            core_rs[2].wait_recv()
        z_out[k] = piece_sum(k, steps[k])
        z_rs[k].start()

    def ref_level():
        total = piece_sum(len(steps), 0)
        all_of(z_in, z_send.at[0], z_recv.at[0]).wait_recv()
        for k in range(len(steps)):
            total = total + z_in[k]
        whole[core, level_piece(side, level)] = total
        for copy in z_ag:
            copy.start()
        y_ag[len(steps)].start()

    def ref_back(k):
        z_ag[k].wait_recv()
        y_ag[k].start()
        if k == len(steps) - 1:
            core_ag[0].start()

    def ref_other():
        all_of(y_out, y_send.at[1], y_recv.at[1]).wait_recv()
        core_ag[1].start()

    ref_core()
    tail_core()

    smalls[0].wait()
    smalls[1].wait()

    for d in range(kept):
        for a in range(chips_az):
            row = (d * chips_az + a) * tiles
            for i in range(2):
                spots[i, row : row + tiles, :chips_rg] = shifts_ref[i, d, a]
                spots[2 + i, row : row + tiles, :chips_rg] = fractions_ref[i, d, a]
    spot_rows = kept * chips_az * tiles
    first_tap = MARGIN - TAP_COUNT // 2 + 1
    at = wide(spot_rows)
    for r in range(chips_rg):
        values = [
            jnp.broadcast_to(spots[i, 0:spot_rows, r : r + 1], (spot_rows, LANES)) for i in range(4)
        ]
        line_tap = ((LANES - at) & (LANES - 1)) - (values[0] + first_tap)
        line_base[r, 0:spot_rows, :] = tap_weights(line_tap, values[2])
        col_tap = at - (values[1] + (first_tap + HALO - MARGIN))
        col_base[r, 0:spot_rows, :] = tap_weights(col_tap, values[3])

    low_lane = wide(CHIP_SIZE) < CHIP_SIZE

    def halves(count):
        return wide(count) < CHIP_SIZE

    def chip_column(d, t, r, slot):
        row0 = r * CHIP_SIZE
        window = pl.ds(row0, WINDOW)

        def base(ref, a):
            return ref[r, pl.ds((d * chips_az + a) * tiles + t, 1), :]

        partial = [None] * chips_az
        reach = CHIP_SIZE + 2 * MARGIN
        for a in range(0, chips_az - 1, 2):
            b = a // 2
            span = slice(b * LANES, b * LANES + BAND)
            image = jnp.concatenate([frame[d, t, c, window, span] for c in range(2)], axis=0)
            first = spread(base(line_base, a), reach, 0)
            second = spread(base(line_base, a + 1), BAND - CHIP_SIZE, CHIP_SIZE)
            shared = reach - CHIP_SIZE
            matrix = jnp.concatenate(
                [
                    jnp.where(halves(CHIP_SIZE), first[:CHIP_SIZE], 0.0),
                    jnp.where(halves(shared), first[CHIP_SIZE:], second[:shared]),
                    jnp.where(halves(BAND - reach), 0.0, second[shared:]),
                ],
                axis=0,
            ).astype(bf16)
            out = jnp.dot(image, matrix, preferred_element_type=f32)
            re, im = out[:WINDOW], out[WINDOW:]
            left = halves(WINDOW)
            partial[a] = jnp.where(left, re, pltpu.roll(im, CHIP_SIZE, 1)).astype(bf16)
            partial[a + 1] = jnp.where(left, pltpu.roll(re, CHIP_SIZE, 1), im).astype(bf16)
        if chips_az % 2:
            a = chips_az - 1
            span = slice(a * CHIP_SIZE, a * CHIP_SIZE + reach)
            row = base(line_base, a)
            left = halves(reach)
            top = jnp.where(left, spread(row, reach, 0), 0.0).astype(bf16)
            bottom = jnp.where(left, 0.0, spread(row, reach, CHIP_SIZE)).astype(bf16)
            partial[a] = (
                jnp.dot(frame[d, t, 0, window, span], top, preferred_element_type=f32)
                + jnp.dot(frame[d, t, 1, window, span], bottom, preferred_element_type=f32)
            ).astype(bf16)
        for a in range(chips_az):
            matrix = spread(base(col_base, a), CHIP_SIZE, 0)[:, :WINDOW].astype(bf16)
            out = jnp.dot(matrix, partial[a], preferred_element_type=f32).astype(bf16)
            if slot is not None:
                unit = (r * chips_az + a) * chip_units
                sent[slot, pl.ds(unit, chip_units)] = out.reshape(chip_units, PACK, LANES)
            out = out.astype(f32)
            series[t, d + t, a, pl.ds(row0, CHIP_SIZE), :] = out
            power = jnp.sum((out * out).reshape(GROUP, GROUP, LANES), axis=0)
            totals[1 + 2 * kept + d, r, pl.ds((t * group_rows + a) * GROUP, GROUP), :] = power

    def resample(i, first, last):
        d, t = order[i]

        for j in range(first, last):
            chip_column(d, t, (j + 1) % chips_rg, i if i < 2 else None)

    inside_cols = chips_rg - 2
    column = chips_az * chip_units
    outward = []
    for r in range(chips_rg):
        span = pl.ds(r * column, column)
        outward.append(
            remote(sent.at[0, span], got.at[0, span], next_send.at[0], next_recv.at[0], {"date": peer})
        )

    def outward_start(first, last):
        @pl.when(has_peer)
        def _():
            for r in range(first, last):
                outward[(r + 1) % chips_rg].start()

    def outward_all():
        return remote(sent.at[0], got.at[0], next_send.at[0], next_recv.at[0], {"date": peer})

    inward = remote(
        sent.at[1], got.at[1], next_send.at[1], next_recv.at[1], device(level, side, 1 - core)
    )

    resample(0, 0, inside_cols)
    ref_side(0)
    edge_wait(0)
    resample(0, inside_cols, chips_rg)
    ref_side(1)
    outward_start(0, EARLY)
    resample(1, 0, inside_cols)
    for k in range(2, len(steps)):
        ref_side(k)
    outward_start(EARLY, 3)
    edge_wait(1)
    resample(1, inside_cols, chips_rg)
    inward.start()
    tail_side()
    outward_start(3, chips_rg)
    resample(2, 0, inside_cols)
    ref_level()
    edge_wait(2)
    resample(2, inside_cols, chips_rg)
    resample(3, 0, inside_cols)
    edge_wait(3)
    resample(3, inside_cols, chips_rg)

    looks_rg = cols // LOOK_RG
    look_rows = rows // LOOK_AZ

    def pick_rows(t, pos, a, s):
        return series[t, pos, a, pl.ds(s, looks_rg, stride=LOOK_RG), :]

    def look(t, early, wanted):
        for a in range(chips_az):
            sums = [jnp.zeros((looks_rg, LANES), f32) for _ in range(2 + len(wanted))]
            for s in range(LOOK_RG):
                first = pick_rows(t, early, a, s)
                second = pick_rows(t, early + 1, a, s)
                sums[0] = sums[0] + first * second
                sums[1] = sums[1] + first * pltpu.roll(second, CHIP_SIZE, 1)
                for i, pos in enumerate(wanted):
                    value = pick_rows(t, pos, a, s)
                    sums[2 + i] = sums[2 + i] + value * value
            span = slice(a * LANES, (a + 1) * LANES)
            row = pl.multiple_of((early * tiles + t) * looks_rg, GROUP)
            for c in range(2):
                cross_sums[c, pl.ds(row, looks_rg), span] = sums[c]
            for i, pos in enumerate(wanted):
                row = pl.multiple_of((pos * tiles + t) * looks_rg, GROUP)
                powers[pl.ds(row, looks_rg), span] = sums[2 + i]

    def unpack(i, t, pos):
        def body(j, carry):
            for a in range(chips_az):
                unit = (j * chips_az + a) * chip_units
                value = got[i, pl.ds(unit, chip_units)].reshape(CHIP_SIZE, LANES)
                row = pl.multiple_of(j * CHIP_SIZE, CHIP_SIZE)
                series[t, pos, a, pl.ds(row, CHIP_SIZE), :] = value.astype(f32)
            return carry

        lax.fori_loop(0, chips_rg, body, 0)

    look(1 - core, 1 - core, (1 - core, 2 - core))

    def build_selectors(a, carry):
        line = lax.broadcasted_iota(jnp.int32, (LANES, LANES), 0)
        y = lax.broadcasted_iota(jnp.int32, (LANES, LANES), 1)
        gap = a * CHIP_SIZE + (line & (CHIP_SIZE - 1)) - LOOK_AZ * y
        hit = (gap >= 0) & (gap < LOOK_AZ)
        span = pl.ds(pl.multiple_of(a * LANES, LANES), LANES)
        selectors[0, span, :] = jnp.where(hit, 1.0, 0.0).astype(bf16)
        selectors[1, span, :] = jnp.where(
            hit, jnp.where(line < CHIP_SIZE, -1.0, 1.0), 0.0
        ).astype(bf16)
        return carry

    lax.fori_loop(0, chips_az, build_selectors, 0)
    source = lax.broadcasted_iota(jnp.int32, gather.shape, 0)
    target = lax.broadcasted_iota(jnp.int32, gather.shape, 1)
    gap = source - target * LANES
    gather[...] = jnp.where((gap >= 0) & (gap < LANES), 1.0, 0.0).astype(bf16)

    def correlate(t, first, count):
        for j in range(count):
            chip = first + j
            a = chip % chips_az
            r = chip // chips_az
            row = pl.multiple_of(r * CHIP_SIZE, CHIP_SIZE)
            to = pl.ds(pl.multiple_of((t * group_rows + a) * GROUP, GROUP), GROUP)
            sums = [None] * (1 + 2 * kept)
            for g in range(chip_units):
                ref = whole[t, chip * chip_units + g].astype(f32)
                turned = pltpu.roll(ref, CHIP_SIZE, 1)
                terms = [ref * ref]
                for d in range(kept):
                    value = series[t, d + t, a, pl.ds(row + g * PACK, PACK), :]
                    terms += [ref * value, turned * value]
                for k, term in enumerate(terms):
                    term = term[:GROUP] + term[GROUP:]
                    sums[k] = term if sums[k] is None else sums[k] + term
            for k, value in enumerate(sums):
                totals[k, r, to, :] = value

    look(core, core, (core, 1 + core))
    inward.wait_recv()
    unpack(1, core, 2 * (1 - core))
    look(core, 1 - core, (2 * (1 - core),))

    for k in range(2):
        ref_back(k)
    tail_level()

    @pl.when(has_peer)
    def _():
        outward_all().wait_recv()
        unpack(0, 1 - core, 2 * core)

    @pl.when(jnp.logical_not(has_peer))
    def _():
        series[1 - core, 2 * core] = jnp.zeros(series.shape[2:], f32)

    look(1 - core, core, (2 * core,))

    summed = [split_dot(cross_sums[c], selectors[c]) for c in range(2)]
    power = split_dot(powers[...], selectors[0])
    count = kept * tiles * looks_rg
    skip = tiles * looks_rg
    scale = jnp.sqrt((power[:count] + epsilon) * (power[skip : skip + count] + epsilon))
    coherence = jnp.concatenate([v / scale for v in summed], axis=0).T
    share = look_rows // n
    for j in range(n):
        out_buf[j] = coherence[j * share : (j + 1) * share]
    coh_in[me] = out_buf[me]
    for o in range(1, n):
        to = lax.rem(me + o, n)
        copy = remote(
            out_buf.at[to], coh_in.at[me], coh_send.at[0], coh_recv.at[0], {"date": to}
        )
        copy.start()

    for k in range(2, len(steps)):
        ref_back(k)
    tail_back()
    tail_chips = chips - tail_first
    correlate(core, side * half_chips, half_chips)
    correlate(core, tail_first, tail_chips)
    core_ag[0].wait_recv()
    correlate(1 - core, side * half_chips, half_chips)
    core_ag[2].wait_recv()
    correlate(1 - core, tail_first, tail_chips)
    ref_other()
    kinds = totals.shape[0]

    def finish(t):
        sign = jnp.where(wide(group_rows) < CHIP_SIZE, 1.0, -1.0).astype(f32)
        folded = []
        for k in range(kinds):
            line = []
            for r in range(chips_rg):
                total = None
                for s in range(GROUP):
                    at = pl.ds(t * (group_rows * GROUP) + s, group_rows, stride=GROUP)
                    value = totals[k, r, at, :]
                    total = value if total is None else total + value
                if 1 <= k <= 2 * kept and k % 2 == 0:
                    total = total * sign
                line.append(total)
            folded.append(jnp.concatenate(line, axis=1))
        sums = split_dot(jnp.concatenate(folded, axis=0), gather[...])
        sums = [sums[k * group_rows : (k + 1) * group_rows] for k in range(kinds)]
        for d in range(kept):
            scale = jnp.sqrt((sums[0] + epsilon) * (sums[1 + 2 * kept + d] + epsilon))
            for c in range(2):
                value = sums[1 + 2 * d + c] / scale
                for a in range(chips_az):
                    corr_ref[c, d, a, pl.ds(t, 1), :] = value[a : a + 1, :chips_rg]

    correlate(core, (1 - side) * half_chips, half_chips)
    finish(core)

    others = pl.ds(0, n - 1)
    relays = remote(
        out_buf.at[others], coh_in.at[others], coh_send.at[0], coh_recv.at[0], {"date": me}
    )
    relays.wait_recv()
    pairs = n * kept
    lane_n = wide(n)
    for y in range(share):
        value = coh_in[:, y, :]
        ordered[y, pl.ds(0, n, stride=2), :] = value
        ordered[y, pl.ds(1, n, stride=2), :] = pltpu.roll(value, LANES - tiles * looks_rg, 1)
    lane_p = wide(pairs)
    for y in range(share):
        first = (lane_p & (2 * looks_rg - 1)) < looks_rg
        value = jnp.where(first, ordered[y, 0:pairs, :], ordered[y, 1 : pairs + 1, :]).T
        for c in range(2):
            for t in range(tiles):
                row = c * kept * tiles * looks_rg + t * looks_rg
                coh_ref[c, t, y] = value[row : row + looks_rg, : pairs - 1]

    core_ag[1].wait_recv()
    correlate(1 - core, (1 - side) * half_chips, half_chips)
    finish(1 - core)

    relays.wait_send()
    inward.wait_send()
    for ref, sem in (
        (cand.at[1 - core], core_send.at[0]),
        (whole.at[core], core_send.at[1]),
        (y_out, y_send.at[0]),
        (y_out, y_send.at[1]),
        (over, y_send.at[2]),
        (z_out, z_send.at[0]),
        (z_out, z_send.at[1]),
        (across_in, z_send.at[2]),
        (across_in, z_send.at[3]),
    ):
        all_of(ref, sem, sem).wait_send()

    @pl.when(has_peer)
    def _():
        outward_all().wait_send()

    rim = frame.at[:, :, :, 0:HALO, :]

    @pl.when(has_high)
    def _():
        all_of(rim, edge_send.at[0], edge_send.at[0]).wait_send()

    @pl.when(has_low)
    def _():
        all_of(rim, edge_send.at[1], edge_send.at[1]).wait_send()


def per_device(n, strips, acquisitions, shifts, fractions, ref_dates):
    kept, tiles, _, all_rows, cols = acquisitions.shape
    rows = all_rows - 2 * MARGIN
    chips_az, chips_rg = shifts.shape[3:]
    chips = chips_az * chips_rg
    units = chips * CHIP_SIZE // PACK
    levels = n // (CORES * SIDES)
    piece = max(units * SHARE // 100 // levels, 1)
    half_units = piece * levels
    strip_piece = -(-(units - SIDES * half_units) // levels)
    total_units = SIDES * half_units + levels * strip_piece
    looks_rg = cols // LOOK_RG
    look_rows = rows // LOOK_AZ
    share = look_rows // n
    spot_rows = -(-(kept * chips_az * tiles) // GROUP) * GROUP
    group_rows = -(-chips_az // GROUP) * GROUP
    kinds = 1 + 3 * kept
    f32 = jnp.float32
    bf16 = jnp.bfloat16
    dma = pltpu.SemaphoreType.DMA
    vmem = pl.BlockSpec(memory_space=pltpu.VMEM)
    frames = jnp.swapaxes(acquisitions, 3, 4)
    order = (0, 1, 3, 2, 4)
    coh, corr = pl.pallas_call(
        functools.partial(kernel, n, strips, (tiles, kept, chips_az, chips_rg, rows, cols)),
        out_shape=(
            jax.ShapeDtypeStruct((2, tiles, share, looks_rg, n * kept - 1), f32),
            jax.ShapeDtypeStruct((2, kept, chips_az, tiles, chips_rg), f32),
        ),
        in_specs=[pl.BlockSpec(memory_space=pltpu.HBM)] * 4,
        out_specs=(vmem, vmem),
        scratch_shapes=[
            pltpu.VMEM((kept, tiles, 2, cols + 2 * HALO, all_rows), bf16),
            pltpu.VMEM((2, kept, chips_az, tiles, chips_rg), jnp.int32),
            pltpu.VMEM((2, kept, chips_az, tiles, chips_rg), jnp.int32),
            pltpu.VMEM((1, tiles), jnp.int32),
            pltpu.VMEM((4, spot_rows, LANES), jnp.int32),
            pltpu.VMEM((chips_rg, spot_rows, LANES), f32),
            pltpu.VMEM((chips_rg, spot_rows, LANES), f32),
            pltpu.VMEM((tiles, total_units, PACK, LANES), bf16),
            pltpu.VMEM((total_units, PACK, LANES), bf16),
            pltpu.VMEM((half_units, PACK, LANES), bf16),
            pltpu.VMEM((levels, piece, PACK, LANES), bf16),
            pltpu.VMEM((levels - 1, piece, PACK, LANES), bf16),
            pltpu.VMEM((levels - 1, piece, PACK, LANES), bf16),
            pltpu.VMEM((levels * strip_piece, PACK, LANES), bf16),
            pltpu.VMEM((levels - 1, strip_piece, PACK, LANES), bf16),
            pltpu.VMEM((strip_piece, PACK, LANES), bf16),
            pltpu.VMEM((strip_piece, PACK, LANES), bf16),
            pltpu.VMEM((tiles, total_units, PACK, LANES), bf16),
            pltpu.VMEM((tiles, kept + 1, chips_az, cols, LANES), f32),
            pltpu.VMEM((2, units, PACK, LANES), bf16),
            pltpu.VMEM((2, units, PACK, LANES), bf16),
            pltpu.VMEM((2, kept * tiles * looks_rg, chips_az * LANES), f32),
            pltpu.VMEM(((kept + 1) * tiles * looks_rg, chips_az * LANES), f32),
            pltpu.VMEM((2, chips_az * LANES, LANES), bf16),
            pltpu.VMEM((n, share, LANES), f32),
            pltpu.VMEM((n, share, LANES), f32),
            pltpu.VMEM((share, n * kept + GROUP, LANES), f32),
            pltpu.VMEM((kinds, chips_rg, tiles * group_rows * GROUP, LANES), f32),
            pltpu.VMEM((chips_rg * LANES, LANES), bf16),
            dma((3,)), dma((3,)), dma((2,)), dma((2, 4)), dma((2,)), dma((6,)),
            dma((3,)), dma((3,)), dma((4,)), dma((4,)), dma((levels,)), dma((levels - 1,)),
            dma((2,)), dma((2,)), dma((1,)), dma((1,)),
        ],
        compiler_params=pltpu.CompilerParams(
            collective_id=0, has_side_effects=True, vmem_limit_bytes=50 * 1024 * 1024
        ),
    )(*[pltpu.with_memory_space_constraint(v, pltpu.HBM) for v in (frames, shifts.transpose(order), fractions.transpose(order), ref_dates[None])])
    return (corr.transpose(order), coh.transpose(0, 4, 1, 2, 3))


def solution(mesh):
    return jax.shard_map(
        functools.partial(per_device, mesh.shape["date"], mesh.shape["strip"]),
        mesh=mesh,
        in_specs=(
            P("date", None, None, None, "strip"),
            P(None, "date", None, None, "strip"),
            P(None, "date", None, None, "strip"),
            P(),
        ),
        out_specs=(P(None, "date", None, None, "strip"), P(None, None, None, "date", "strip")),
        check_vma=False,
    )
```
